128 devices in a mesh: lat: 8 (over z, core), lon: 16 (over x, y).
Axes of the slice: x: 4, y: 4, z: 4, core: 2. Of those that a mesh axis runs over, the one named last changes fastest.
Arguments:
- surface: float32 [2048, 16384], P('lat', 'lon'), may hold values from -24 to 24
- bathymetry: float32 [2048, 16384], P('lat', 'lon'), may hold values from 0.1 to 1
- land_sea: int32 [2048, 16384], P('lat', 'lon'), may hold values 0 or 1
- flux_lon: float32 [2048, 16384], P('lat', 'lon'), may hold values from -12 to 12
- flux_lat: float32 [2048, 16384], P('lat', 'lon'), may hold values from -12 to 12
Outputs:
- surface_next: float32 [2048, 16384], P('lat', 'lon')
- flux_lon_next: float32 [2048, 16384], P('lat', 'lon')
- flux_lat_next: float32 [2048, 16384], P('lat', 'lon')
The draws below stay inside these ranges and needn't reach their ends.
All inputs are finite; a program needn't handle non-finite values. No bound on the sum of `land_sea` on one device may be relied on, other than what follows from the above.
Results may differ from the reference program's by a relative error of at most 0.0001.
Values sent between devices are 32-bit elements; how exact they have to be, the bound alone decides.
A program may use at most 64 MiB of HBM per device.

```python
import math
import jax
import jax.numpy as jnp

ITERS = 3
NLAT = 2048
NLON = 16384


def ramp_field(key, scale):
    rows = jnp.arange(NLAT, dtype=jnp.float32)[:, None] / NLAT
    cols = jnp.arange(NLON, dtype=jnp.float32)[None, :] / NLON
    rough = jnp.clip(jax.random.normal(key, (NLAT, NLON), jnp.float32), -4.0, 4.0)
    growth = jnp.exp(math.log(3.0) * (rows + cols) * 0.5)
    return scale * rough * growth


def draw_surface(key, part):
    return ramp_field(jax.random.fold_in(key, 11), 1.0)


def draw_flux_lon(key, part):
    return ramp_field(jax.random.fold_in(key, 23), 0.5)


def draw_flux_lat(key, part):
    return ramp_field(jax.random.fold_in(key, 37), 0.5)


def plant(values, rng, smallest, largest):
    spot = [jax.random.randint(jax.random.fold_in(rng, axis), (), 0, length) for axis, length in enumerate(values.shape)]
    main_axis = values.shape.index(max(values.shape))
    neighbour = spot[:main_axis] + [(spot[main_axis] + 1) % values.shape[main_axis]] + spot[main_axis + 1:]
    return values.at[tuple(spot)].set(smallest).at[tuple(neighbour)].set(largest)


def steps_of(stream_key, shape, split, smallest, high):
    level, own = 1.0, jax.random.fold_in(stream_key, 6)
    for dim, parts in split:
        steps = jnp.exp(jax.random.uniform(jax.random.fold_in(own, dim), (parts,), jnp.float32, smallest / len(split), high / len(split)))
        level = level * jnp.repeat(steps, shape[dim] // parts).reshape([-1 if axis == dim else 1 for axis in range(len(shape))])
    return level


def setup_inputs(seed: int = 0) -> dict:
    key_list = jax.random.split(jax.random.key(seed), 6)
    surface = draw_surface(jax.random.fold_in(key_list[5], 71), 0)
    bathymetry = jnp.clip(jnp.exp(math.log(1.0) - 2.3025851 * jax.random.uniform(key_list[1], (NLAT, NLON), jnp.float32) ** steps_of(key_list[1], (NLAT, NLON), ((0, 8), (1, 16)), -0.2, 0.2)), 0.1, 1.0)
    land_sea = plant((jax.random.randint(key_list[2], (NLAT, NLON), 0, 5) < 4).astype(jnp.int32), jax.random.fold_in(key_list[2], 1), 0, 1)
    flux_lon = draw_flux_lon(jax.random.fold_in(key_list[5], 71), 0)
    flux_lat = draw_flux_lat(jax.random.fold_in(key_list[5], 71), 0)
    return dict(surface=surface, bathymetry=bathymetry, land_sea=land_sea, flux_lon=flux_lon, flux_lat=flux_lat)


courant = -0.4
dispersion = 40.0
continuity = -0.5


def east(field):
    return jnp.pad(field[:, 1:], ((0, 0), (0, 1)))


def north(field):
    return jnp.pad(field[1:, :], ((0, 1), (0, 0)))


def west(field):
    return jnp.pad(field[:, :-1], ((0, 0), (1, 0)))


def south(field):
    return jnp.pad(field[:-1, :], ((1, 0), (0, 0)))


def divergence(field):
    return field[0] - west(field[0]) + field[1] - south(field[1])


def operate(field, wet, inverse):
    diverge = divergence(field)
    back = jnp.stack([diverge - east(diverge), diverge - north(diverge)])
    return wet * (inverse * field + back)


def reference(surface, bathymetry, land_sea, flux_lon, flux_lat):
    sea = land_sea.astype(jnp.float32)
    wet = jnp.stack([sea * east(sea), sea * north(sea)])
    depth = jnp.stack([0.5 * (bathymetry + east(bathymetry)), 0.5 * (bathymetry + north(bathymetry))])
    slope = jnp.stack([east(surface) - surface, north(surface) - surface])
    start = wet * (jnp.stack([flux_lon, flux_lat]) - courant * depth * slope)
    inverse = 1.0 / (dispersion * depth * depth)
    right_side = wet * inverse * start
    solution = start
    residual = right_side - operate(start, wet, inverse)
    direction = residual
    norm_now = jnp.sum(residual * residual)
    for step in range(ITERS):
        image = operate(direction, wet, inverse)
        alpha = norm_now / jnp.sum(direction * image)
        solution = solution + alpha * direction
        residual = residual - alpha * image
        norm_next = jnp.sum(residual * residual)
        direction = residual + (norm_next / norm_now) * direction
        norm_now = norm_next
    surface_next = surface - continuity * divergence(solution)
    return surface_next, solution[0], solution[1]
```

```python
import jax
import jax.numpy as jnp
from jax import lax
from jax.sharding import PartitionSpec as P

ITERS = 3


courant = -0.4
dispersion = 40.0
continuity = -0.5


def from_behind(value, axis, steps):
    count = lax.axis_size(axis)
    leading, last = (max(0, -steps), min(count, count - steps))
    return lax.ppermute(value, axis, [(source, source + steps) for source in range(leading, last)])


def upper_cells(stacked):
    north_row = from_behind(stacked[:, :1, :], "lat", -1)
    east_col = from_behind(stacked[:, :, :1], "lon", -1)
    eastern = jnp.concatenate([stacked[:, :, 1:], east_col], axis=2)
    northern = jnp.concatenate([stacked[:, 1:, :], north_row], axis=1)
    return (eastern, northern)


def lower_fluxes(field):
    south_row = from_behind(field[:, -1:, :], "lat", 1)
    west_col = from_behind(field[:, :, -1:], "lon", 1)
    western = jnp.concatenate([west_col, field[:, :, :-1]], axis=2)
    southern = jnp.concatenate([south_row, field[:, :-1, :]], axis=1)
    return (western, southern)


def divergence(field):
    western, southern = lower_fluxes(field)
    return field[0] - western[0] + field[1] - southern[1]


def gradient_back(field):
    diverge = divergence(field)
    eastern, northern = upper_cells(diverge[None])
    return jnp.stack([diverge - eastern[0], diverge - northern[0]])


def operate(field, wet, inverse):
    return wet * (inverse * field + gradient_back(field))


def sums(*pairs):
    local = jnp.stack([jnp.sum(x * y) for x, y in pairs])
    return lax.psum(local, ("lat", "lon"))


def per_device(surface, bathymetry, land_sea, flux_lon, flux_lat):
    sea = land_sea.astype(jnp.float32)
    cells = jnp.stack([surface, bathymetry, sea])
    eastern, northern = upper_cells(cells)
    wet = jnp.stack([sea * eastern[2], sea * northern[2]])
    depth = jnp.stack([0.5 * (bathymetry + eastern[1]), 0.5 * (bathymetry + northern[1])])
    slope = jnp.stack([eastern[0] - surface, northern[0] - surface])
    start = wet * (jnp.stack([flux_lon, flux_lat]) - courant * depth * slope)
    inverse = 1.0 / (dispersion * depth * depth)
    right_side = wet * inverse * start
    solution = start
    residual = right_side - operate(start, wet, inverse)
    applied = operate(residual, wet, inverse)
    norm_now, curve = sums((residual, residual), (residual, applied))
    direction, image = residual, applied
    for step in range(ITERS):
        alpha = norm_now / curve
        solution = solution + alpha * direction
        if step == ITERS - 1:
            break
        residual = residual - alpha * image
        applied = operate(residual, wet, inverse)
        norm_next, r_ar, r_ap = sums((residual, residual), (residual, applied), (residual, image))
        beta = norm_next / norm_now
        curve = r_ar + 2.0 * beta * r_ap + beta * beta * curve
        direction = residual + beta * direction
        image = applied + beta * image
        norm_now = norm_next
    surface_next = surface - continuity * divergence(solution)
    return (surface_next, solution[0], solution[1])


def solution(mesh):
    in_specs = (P("lat", "lon"), P("lat", "lon"), P("lat", "lon"), P("lat", "lon"), P("lat", "lon"))
    out_specs = (P("lat", "lon"), P("lat", "lon"), P("lat", "lon"))
    return jax.shard_map(
        per_device, mesh=mesh, in_specs=in_specs, out_specs=out_specs, check_vma=False
    )
```

```python
import jax
import jax.numpy as jnp
from jax import lax
from jax.sharding import PartitionSpec as P

ITERS = 3


courant = -0.4
dispersion = 40.0
continuity = -0.5


def from_behind(value, axis, steps):
    count = lax.axis_size(axis)
    leading, last = (max(0, -steps), min(count, count - steps))
    return lax.ppermute(value, axis, [(source, source + steps) for source in range(leading, last)])


def upper_cells(stacked):
    north_row = from_behind(stacked[:, :1, :], "lat", -1)
    east_col = from_behind(stacked[:, :, :1], "lon", -1)
    eastern = jnp.concatenate([stacked[:, :, 1:], east_col], axis=2)
    northern = jnp.concatenate([stacked[:, 1:, :], north_row], axis=1)
    return (eastern, northern)


def lower_fluxes(field):
    south_row = from_behind(field[:, -1:, :], "lat", 1)
    west_col = from_behind(field[:, :, -1:], "lon", 1)
    western = jnp.concatenate([west_col, field[:, :, :-1]], axis=2)
    southern = jnp.concatenate([south_row, field[:, :-1, :]], axis=1)
    return (western, southern)


def divergence(field):
    western, southern = lower_fluxes(field)
    return field[0] - western[0] + field[1] - southern[1]


def gradient_back(field):
    diverge = divergence(field)
    eastern, northern = upper_cells(diverge[None])
    return jnp.stack([diverge - eastern[0], diverge - northern[0]])


def operate(field, wet, inverse):
    return wet * (inverse * field + gradient_back(field))


def exchange(value, axis, mask):
    return lax.ppermute(value, axis, [(i, i ^ mask) for i in range(lax.axis_size(axis))])


def quad_sum(value, axis, step):
    first = exchange(value, axis, step)
    second = exchange(value, axis, 2 * step)
    third = exchange(value, axis, 3 * step)
    return (value + first) + (second + third)


def total(value, axis):
    count, step = lax.axis_size(axis), 1
    while count >= 4:
        value = quad_sum(value, axis, step)
        count, step = count // 4, step * 4
    if count == 2:
        value = value + exchange(value, axis, step)
    return value


def sums(*pairs):
    local = jnp.stack([jnp.sum(x * y) for x, y in pairs])
    return total(total(local, "lon"), "lat")


def per_device(surface, bathymetry, land_sea, flux_lon, flux_lat):
    sea = land_sea.astype(jnp.float32)
    cells = jnp.stack([surface, bathymetry, sea])
    eastern, northern = upper_cells(cells)
    wet = jnp.stack([sea * eastern[2], sea * northern[2]])
    depth = jnp.stack([0.5 * (bathymetry + eastern[1]), 0.5 * (bathymetry + northern[1])])
    slope = jnp.stack([eastern[0] - surface, northern[0] - surface])
    start = wet * (jnp.stack([flux_lon, flux_lat]) - courant * depth * slope)
    inverse = 1.0 / (dispersion * depth * depth)
    right_side = wet * inverse * start
    solution = start
    residual = right_side - operate(start, wet, inverse)
    applied = operate(residual, wet, inverse)
    norm_now, curve = sums((residual, residual), (residual, applied))
    direction, image = residual, applied
    for step in range(ITERS):
        alpha = norm_now / curve
        solution = solution + alpha * direction
        if step == ITERS - 1:
            break
        residual = residual - alpha * image
        applied = operate(residual, wet, inverse)
        norm_next, r_ar, r_ap = sums((residual, residual), (residual, applied), (residual, image))
        beta = norm_next / norm_now
        curve = r_ar + 2.0 * beta * r_ap + beta * beta * curve
        direction = residual + beta * direction
        image = applied + beta * image
        norm_now = norm_next
    surface_next = surface - continuity * divergence(solution)
    return (surface_next, solution[0], solution[1])


def solution(mesh):
    in_specs = (P("lat", "lon"), P("lat", "lon"), P("lat", "lon"), P("lat", "lon"), P("lat", "lon"))
    out_specs = (P("lat", "lon"), P("lat", "lon"), P("lat", "lon"))
    return jax.shard_map(
        per_device, mesh=mesh, in_specs=in_specs, out_specs=out_specs, check_vma=False
    )
```

```python
import jax
import jax.numpy as jnp
from jax import lax
from jax.sharding import PartitionSpec as P

ITERS = 3
MARGIN_ROWS = 8
MARGIN_COLS = 8


courant = -0.4
dispersion = 40.0
continuity = -0.5


def from_behind(value, axis, steps):
    count = lax.axis_size(axis)
    leading, last = (max(0, -steps), min(count, count - steps))
    return lax.ppermute(value, axis, [(source, source + steps) for source in range(leading, last)])


def grow(stacked):
    rows, cols = MARGIN_ROWS, MARGIN_COLS
    above = from_behind(stacked[:, :rows, :], "lat", -1)
    below = from_behind(stacked[:, -rows:, :], "lat", 1)
    stacked = jnp.concatenate([below, stacked, above], axis=1)
    right = from_behind(stacked[:, :, :cols], "lon", -1)
    left = from_behind(stacked[:, :, -cols:], "lon", 1)
    return jnp.concatenate([left, stacked, right], axis=2)


def east(field):
    return jnp.pad(field[..., :, 1:], [(0, 0)] * (field.ndim - 1) + [(0, 1)])


def north(field):
    return jnp.pad(field[..., 1:, :], [(0, 0)] * (field.ndim - 2) + [(0, 1), (0, 0)])


def west(field):
    return jnp.pad(field[..., :, :-1], [(0, 0)] * (field.ndim - 1) + [(1, 0)])


def south(field):
    return jnp.pad(field[..., :-1, :], [(0, 0)] * (field.ndim - 2) + [(1, 0), (0, 0)])


def divergence(field):
    return field[0] - west(field[0]) + field[1] - south(field[1])


def operate(field, wet, inverse):
    diverge = divergence(field)
    back = jnp.stack([diverge - east(diverge), diverge - north(diverge)])
    return wet * (inverse * field + back)


def exchange(value, axis, mask):
    return lax.ppermute(value, axis, [(i, i ^ mask) for i in range(lax.axis_size(axis))])


def quad_sum(value, axis, step):
    first = exchange(value, axis, step)
    second = exchange(value, axis, 2 * step)
    third = exchange(value, axis, 3 * step)
    return (value + first) + (second + third)


def total(value, axis):
    count, step = lax.axis_size(axis), 1
    while count >= 4:
        value = quad_sum(value, axis, step)
        count, step = count // 4, step * 4
    if count == 2:
        value = value + exchange(value, axis, step)
    return value


def interior(field):
    rows, cols = MARGIN_ROWS, MARGIN_COLS
    return field[..., rows:-rows, cols:-cols]


def sums(*pairs):
    local = jnp.stack([jnp.sum(interior(x) * interior(y)) for x, y in pairs])
    return total(total(local, "lon"), "lat")


def per_device(surface, bathymetry, land_sea, flux_lon, flux_lat):
    sea = land_sea.astype(jnp.float32)
    grown = grow(jnp.stack([surface, bathymetry, sea, flux_lon, flux_lat]))
    surface_x, bathymetry_x, sea_x = grown[0], grown[1], grown[2]
    wet = jnp.stack([sea_x * east(sea_x), sea_x * north(sea_x)])
    depth = jnp.stack([0.5 * (bathymetry_x + east(bathymetry_x)), 0.5 * (bathymetry_x + north(bathymetry_x))])
    slope = jnp.stack([east(surface_x) - surface_x, north(surface_x) - surface_x])
    start = wet * (grown[3:] - courant * depth * slope)
    inverse = jnp.where(depth > 0, 1.0 / (dispersion * depth * depth), 0.0)
    right_side = wet * inverse * start
    solution = start
    residual = right_side - operate(start, wet, inverse)
    applied = operate(residual, wet, inverse)
    norm_now, curve = sums((residual, residual), (residual, applied))
    direction, image = residual, applied
    for step in range(ITERS):
        alpha = norm_now / curve
        solution = solution + alpha * direction
        if step == ITERS - 1:
            break
        residual = residual - alpha * image
        applied = operate(residual, wet, inverse)
        norm_next, r_ar, r_ap = sums((residual, residual), (residual, applied), (residual, image))
        beta = norm_next / norm_now
        curve = r_ar + 2.0 * beta * r_ap + beta * beta * curve
        direction = residual + beta * direction
        image = applied + beta * image
        norm_now = norm_next
    surface_next = interior(surface_x - continuity * divergence(solution))
    solution = interior(solution)
    return (surface_next, solution[0], solution[1])


def solution(mesh):
    in_specs = (P("lat", "lon"), P("lat", "lon"), P("lat", "lon"), P("lat", "lon"), P("lat", "lon"))
    out_specs = (P("lat", "lon"), P("lat", "lon"), P("lat", "lon"))
    return jax.shard_map(
        per_device, mesh=mesh, in_specs=in_specs, out_specs=out_specs, check_vma=False
    )
```

```python
import functools

import jax
import jax.numpy as jnp
from jax import lax
from jax.experimental import pallas as pl
from jax.experimental.pallas import tpu as pltpu
from jax.sharding import PartitionSpec as P

MESH = pl.DeviceIdType.MESH

ITERS = 3
MARGIN_ROWS = 8
MARGIN_COLS = 8


courant = -0.4
dispersion = 40.0
continuity = -0.5


def from_behind(value, axis, steps):
    count = lax.axis_size(axis)
    leading, last = (max(0, -steps), min(count, count - steps))
    return lax.ppermute(value, axis, [(source, source + steps) for source in range(leading, last)])


def grow(stacked):
    rows, cols = MARGIN_ROWS, MARGIN_COLS
    above = from_behind(stacked[:, :rows, :], "lat", -1)
    below = from_behind(stacked[:, -rows:, :], "lat", 1)
    stacked = jnp.concatenate([below, stacked, above], axis=1)
    right = from_behind(stacked[:, :, :cols], "lon", -1)
    left = from_behind(stacked[:, :, -cols:], "lon", 1)
    return jnp.concatenate([left, stacked, right], axis=2)


def east(field):
    return jnp.pad(field[..., :, 1:], [(0, 0)] * (field.ndim - 1) + [(0, 1)])


def north(field):
    return jnp.pad(field[..., 1:, :], [(0, 0)] * (field.ndim - 2) + [(0, 1), (0, 0)])


def west(field):
    return jnp.pad(field[..., :, :-1], [(0, 0)] * (field.ndim - 1) + [(1, 0)])


def south(field):
    return jnp.pad(field[..., :-1, :], [(0, 0)] * (field.ndim - 2) + [(1, 0), (0, 0)])


def divergence(field):
    return field[0] - west(field[0]) + field[1] - south(field[1])


def operate(field, wet, inverse):
    diverge = divergence(field)
    back = jnp.stack([diverge - east(diverge), diverge - north(diverge)])
    return wet * (inverse * field + back)


def stages_of(sizes):
    stages = []
    for axis in ("lon", "lat"):
        count, stride = sizes[axis], 1
        while count > 1:
            members = 4 if count % 4 == 0 else count
            stages.append((axis, stride, members))
            count, stride = count // members, stride * members
    return tuple(stages)


def reduce_kernel(stages, local_ref, out_ref, parts, got, send_sem, recv_sem):
    me = {"lat": lax.axis_index("lat"), "lon": lax.axis_index("lon")}

    def partner(axis, stride, members, offset):
        own = me[axis]
        digit = (own // stride) % members
        other = own - digit * stride + ((digit + offset) % members) * stride
        return tuple(other if name == axis else me[name] for name in ("lat", "lon"))

    barrier = pltpu.get_barrier_semaphore()
    greeted = 0
    for axis, stride, members in stages:
        for offset in range(1, members):
            pl.semaphore_signal(barrier, inc=1, device_id=partner(axis, stride, members, offset), device_id_type=MESH)
            greeted += 1
    pl.semaphore_wait(barrier, greeted)

    value = local_ref[...]
    for stage, (axis, stride, members) in enumerate(stages):
        parts[stage] = value
        got[stage, 0] = value
        copies = []
        for offset in range(1, members):
            slot = members - offset
            copy = pltpu.make_async_remote_copy(
                src_ref=parts.at[stage],
                dst_ref=got.at[stage, slot],
                send_sem=send_sem.at[stage, offset],
                recv_sem=recv_sem.at[stage, slot],
                device_id=partner(axis, stride, members, offset),
                device_id_type=MESH,
            )
            copy.start()
            copies.append(copy)
        for copy in copies:
            copy.wait()
        digit = (me[axis] // stride) % members
        ordered = [got[stage, (member - digit) % members] for member in range(members)]
        while len(ordered) > 1:
            ordered = [ordered[k] + ordered[k + 1] for k in range(0, len(ordered), 2)]
        value = ordered[0]
    out_ref[...] = value


def all_sum(local):
    sizes = {"lat": lax.axis_size("lat"), "lon": lax.axis_size("lon")}
    stages = stages_of(sizes)
    tile = jnp.zeros((8, 128), jnp.float32).at[0, : local.shape[0]].set(local)
    summed = pl.pallas_call(
        functools.partial(reduce_kernel, stages),
        out_shape=jax.ShapeDtypeStruct((8, 128), jnp.float32),
        in_specs=[pl.BlockSpec(memory_space=pltpu.VMEM)],
        out_specs=pl.BlockSpec(memory_space=pltpu.VMEM),
        scratch_shapes=[
            pltpu.VMEM((len(stages), 8, 128), jnp.float32),
            pltpu.VMEM((len(stages), 4, 8, 128), jnp.float32),
            pltpu.SemaphoreType.DMA((len(stages), 4)),
            pltpu.SemaphoreType.DMA((len(stages), 4)),
        ],
        compiler_params=pltpu.CompilerParams(collective_id=0, has_side_effects=True),
    )(tile)
    return summed[0, : local.shape[0]]


def interior(field):
    rows, cols = MARGIN_ROWS, MARGIN_COLS
    return field[..., rows:-rows, cols:-cols]


def sums(*pairs):
    local = jnp.stack([jnp.sum(interior(x) * interior(y)) for x, y in pairs])
    return all_sum(local)


def per_device(surface, bathymetry, land_sea, flux_lon, flux_lat):
    sea = land_sea.astype(jnp.float32)
    grown = grow(jnp.stack([surface, bathymetry, sea, flux_lon, flux_lat]))
    surface_x, bathymetry_x, sea_x = grown[0], grown[1], grown[2]
    wet = jnp.stack([sea_x * east(sea_x), sea_x * north(sea_x)])
    depth = jnp.stack([0.5 * (bathymetry_x + east(bathymetry_x)), 0.5 * (bathymetry_x + north(bathymetry_x))])
    slope = jnp.stack([east(surface_x) - surface_x, north(surface_x) - surface_x])
    start = wet * (grown[3:] - courant * depth * slope)
    inverse = jnp.where(depth > 0, 1.0 / (dispersion * depth * depth), 0.0)
    right_side = wet * inverse * start
    solution = start
    residual = right_side - operate(start, wet, inverse)
    applied = operate(residual, wet, inverse)
    norm_now, curve = sums((residual, residual), (residual, applied))
    direction, image = residual, applied
    for step in range(ITERS):
        alpha = norm_now / curve
        solution = solution + alpha * direction
        if step == ITERS - 1:
            break
        residual = residual - alpha * image
        applied = operate(residual, wet, inverse)
        norm_next, r_ar, r_ap = sums((residual, residual), (residual, applied), (residual, image))
        beta = norm_next / norm_now
        curve = r_ar + 2.0 * beta * r_ap + beta * beta * curve
        direction = residual + beta * direction
        image = applied + beta * image
        norm_now = norm_next
    surface_next = interior(surface_x - continuity * divergence(solution))
    solution = interior(solution)
    return (surface_next, solution[0], solution[1])


def solution(mesh):
    in_specs = (P("lat", "lon"), P("lat", "lon"), P("lat", "lon"), P("lat", "lon"), P("lat", "lon"))
    out_specs = (P("lat", "lon"), P("lat", "lon"), P("lat", "lon"))
    return jax.shard_map(
        per_device, mesh=mesh, in_specs=in_specs, out_specs=out_specs, check_vma=False
    )
```

```python
import functools

import jax
import jax.numpy as jnp
from jax import lax
from jax.experimental import pallas as pl
from jax.experimental.pallas import tpu as pltpu
from jax.sharding import PartitionSpec as P

MESH = pl.DeviceIdType.MESH

ITERS = 3
MARGIN_ROWS = 8
MARGIN_COLS = 8


courant = -0.4
dispersion = 40.0
continuity = -0.5


def from_behind(value, axis, steps):
    count = lax.axis_size(axis)
    leading, last = (max(0, -steps), min(count, count - steps))
    return lax.ppermute(value, axis, [(source, source + steps) for source in range(leading, last)])


def grow(stacked):
    rows, cols = MARGIN_ROWS, MARGIN_COLS
    above = from_behind(stacked[:, :rows, :], "lat", -1)
    below = from_behind(stacked[:, -rows:, :], "lat", 1)
    stacked = jnp.concatenate([below, stacked, above], axis=1)
    right = from_behind(stacked[:, :, :cols], "lon", -1)
    left = from_behind(stacked[:, :, -cols:], "lon", 1)
    return jnp.concatenate([left, stacked, right], axis=2)


def east(field):
    return jnp.pad(field[..., :, 1:], [(0, 0)] * (field.ndim - 1) + [(0, 1)])


def north(field):
    return jnp.pad(field[..., 1:, :], [(0, 0)] * (field.ndim - 2) + [(0, 1), (0, 0)])


def west(field):
    return jnp.pad(field[..., :, :-1], [(0, 0)] * (field.ndim - 1) + [(1, 0)])


def south(field):
    return jnp.pad(field[..., :-1, :], [(0, 0)] * (field.ndim - 2) + [(1, 0), (0, 0)])


def divergence(field):
    return field[0] - west(field[0]) + field[1] - south(field[1])


def operate(field, wet, inverse):
    diverge = divergence(field)
    back = jnp.stack([diverge - east(diverge), diverge - north(diverge)])
    return wet * (inverse * field + back)


def stages_of(sizes):
    return tuple((axis, 1, sizes[axis]) for axis in ("lon", "lat") if sizes[axis] > 1)


def reduce_kernel(stages, local_ref, out_ref, parts, got, send_sem, recv_sem):
    me = {"lat": lax.axis_index("lat"), "lon": lax.axis_index("lon")}

    def partner(axis, stride, members, offset):
        own = me[axis]
        digit = (own // stride) % members
        other = own - digit * stride + ((digit + offset) % members) * stride
        return tuple(other if name == axis else me[name] for name in ("lat", "lon"))

    barrier = pltpu.get_barrier_semaphore()
    greeted = 0
    for axis, stride, members in stages:
        for offset in range(1, members):
            pl.semaphore_signal(barrier, inc=1, device_id=partner(axis, stride, members, offset), device_id_type=MESH)
            greeted += 1
    pl.semaphore_wait(barrier, greeted)

    value = local_ref[...]
    for stage, (axis, stride, members) in enumerate(stages):
        parts[stage] = value
        got[stage, 0] = value
        copies = []
        for offset in range(1, members):
            slot = members - offset
            copy = pltpu.make_async_remote_copy(
                src_ref=parts.at[stage],
                dst_ref=got.at[stage, slot],
                send_sem=send_sem.at[stage, offset],
                recv_sem=recv_sem.at[stage, slot],
                device_id=partner(axis, stride, members, offset),
                device_id_type=MESH,
            )
            copy.start()
            copies.append(copy)
        for copy in copies:
            copy.wait()
        digit = (me[axis] // stride) % members
        ordered = [got[stage, (member - digit) % members] for member in range(members)]
        while len(ordered) > 1:
            ordered = [ordered[k] + ordered[k + 1] for k in range(0, len(ordered), 2)]
        value = ordered[0]
    out_ref[...] = value


def all_sum(local):
    sizes = {"lat": lax.axis_size("lat"), "lon": lax.axis_size("lon")}
    stages = stages_of(sizes)
    widest = max(members for _, _, members in stages)
    tile = jnp.zeros((8, 128), jnp.float32).at[0, : local.shape[0]].set(local)
    summed = pl.pallas_call(
        functools.partial(reduce_kernel, stages),
        out_shape=jax.ShapeDtypeStruct((8, 128), jnp.float32),
        in_specs=[pl.BlockSpec(memory_space=pltpu.VMEM)],
        out_specs=pl.BlockSpec(memory_space=pltpu.VMEM),
        scratch_shapes=[
            pltpu.VMEM((len(stages), 8, 128), jnp.float32),
            pltpu.VMEM((len(stages), widest, 8, 128), jnp.float32),
            pltpu.SemaphoreType.DMA((len(stages), widest)),
            pltpu.SemaphoreType.DMA((len(stages), widest)),
        ],
        compiler_params=pltpu.CompilerParams(collective_id=0, has_side_effects=True),
    )(tile)
    return summed[0, : local.shape[0]]


def interior(field):
    rows, cols = MARGIN_ROWS, MARGIN_COLS
    return field[..., rows:-rows, cols:-cols]


def sums(*pairs):
    local = jnp.stack([jnp.sum(interior(x) * interior(y)) for x, y in pairs])
    return all_sum(local)


def per_device(surface, bathymetry, land_sea, flux_lon, flux_lat):
    sea = land_sea.astype(jnp.float32)
    grown = grow(jnp.stack([surface, bathymetry, sea, flux_lon, flux_lat]))
    surface_x, bathymetry_x, sea_x = grown[0], grown[1], grown[2]
    wet = jnp.stack([sea_x * east(sea_x), sea_x * north(sea_x)])
    depth = jnp.stack([0.5 * (bathymetry_x + east(bathymetry_x)), 0.5 * (bathymetry_x + north(bathymetry_x))])
    slope = jnp.stack([east(surface_x) - surface_x, north(surface_x) - surface_x])
    start = wet * (grown[3:] - courant * depth * slope)
    inverse = jnp.where(depth > 0, 1.0 / (dispersion * depth * depth), 0.0)
    right_side = wet * inverse * start
    solution = start
    residual = right_side - operate(start, wet, inverse)
    applied = operate(residual, wet, inverse)
    norm_now, curve = sums((residual, residual), (residual, applied))
    direction, image = residual, applied
    for step in range(ITERS):
        alpha = norm_now / curve
        solution = solution + alpha * direction
        if step == ITERS - 1:
            break
        residual = residual - alpha * image
        applied = operate(residual, wet, inverse)
        norm_next, r_ar, r_ap = sums((residual, residual), (residual, applied), (residual, image))
        beta = norm_next / norm_now
        curve = r_ar + 2.0 * beta * r_ap + beta * beta * curve
        direction = residual + beta * direction
        image = applied + beta * image
        norm_now = norm_next
    surface_next = interior(surface_x - continuity * divergence(solution))
    solution = interior(solution)
    return (surface_next, solution[0], solution[1])


def solution(mesh):
    in_specs = (P("lat", "lon"), P("lat", "lon"), P("lat", "lon"), P("lat", "lon"), P("lat", "lon"))
    out_specs = (P("lat", "lon"), P("lat", "lon"), P("lat", "lon"))
    return jax.shard_map(
        per_device, mesh=mesh, in_specs=in_specs, out_specs=out_specs, check_vma=False
    )
```

```python
import functools

import jax
import jax.numpy as jnp
from jax import lax
from jax.experimental import pallas as pl
from jax.experimental.pallas import tpu as pltpu
from jax.sharding import PartitionSpec as P

MESH = pl.DeviceIdType.MESH

ITERS = 3
MARGIN_ROWS = 8
MARGIN_COLS = 8


courant = -0.4
dispersion = 40.0
continuity = -0.5


def from_behind(value, axis, steps):
    count = lax.axis_size(axis)
    leading, last = (max(0, -steps), min(count, count - steps))
    return lax.ppermute(value, axis, [(source, source + steps) for source in range(leading, last)])


def grow(fields):
    rows, cols = MARGIN_ROWS, MARGIN_COLS
    above = from_behind(jnp.stack([f[:rows] for f in fields]), "lat", -1)
    below = from_behind(jnp.stack([f[-rows:] for f in fields]), "lat", 1)
    tall = [jnp.concatenate([f, above[k], below[k]], axis=0) for k, f in enumerate(fields)]
    right = from_behind(jnp.stack([f[:, :cols] for f in tall]), "lon", -1)
    left = from_behind(jnp.stack([f[:, -cols:] for f in tall]), "lon", 1)
    return [jnp.concatenate([f, right[k], left[k]], axis=1) for k, f in enumerate(tall)]


def east(field):
    return jnp.roll(field, -1, axis=-1)


def north(field):
    return jnp.roll(field, -1, axis=-2)


def west(field):
    return jnp.roll(field, 1, axis=-1)


def south(field):
    return jnp.roll(field, 1, axis=-2)


def divergence(field):
    return field[0] - west(field[0]) + field[1] - south(field[1])


def operate(field, wet, inverse):
    diverge = divergence(field)
    back = jnp.stack([diverge - east(diverge), diverge - north(diverge)])
    return wet * (inverse * field + back)


def stages_of(sizes):
    return tuple((axis, 1, sizes[axis]) for axis in ("lon", "lat") if sizes[axis] > 1)


def reduce_kernel(stages, local_ref, out_ref, parts, got, send_sem, recv_sem):
    me = {"lat": lax.axis_index("lat"), "lon": lax.axis_index("lon")}

    def partner(axis, stride, members, offset):
        own = me[axis]
        digit = (own // stride) % members
        other = own - digit * stride + ((digit + offset) % members) * stride
        return tuple(other if name == axis else me[name] for name in ("lat", "lon"))

    barrier = pltpu.get_barrier_semaphore()
    greeted = 0
    for axis, stride, members in stages:
        for offset in range(1, members):
            pl.semaphore_signal(barrier, inc=1, device_id=partner(axis, stride, members, offset), device_id_type=MESH)
            greeted += 1
    pl.semaphore_wait(barrier, greeted)

    value = local_ref[...]
    for stage, (axis, stride, members) in enumerate(stages):
        parts[stage] = value
        got[stage, 0] = value
        copies = []
        for offset in range(1, members):
            slot = members - offset
            copy = pltpu.make_async_remote_copy(
                src_ref=parts.at[stage],
                dst_ref=got.at[stage, slot],
                send_sem=send_sem.at[stage, offset],
                recv_sem=recv_sem.at[stage, slot],
                device_id=partner(axis, stride, members, offset),
                device_id_type=MESH,
            )
            copy.start()
            copies.append(copy)
        for copy in copies:
            copy.wait()
        digit = (me[axis] // stride) % members
        ordered = [got[stage, (member - digit) % members] for member in range(members)]
        while len(ordered) > 1:
            ordered = [ordered[k] + ordered[k + 1] for k in range(0, len(ordered), 2)]
        value = ordered[0]
    out_ref[...] = value


def all_sum(local):
    sizes = {"lat": lax.axis_size("lat"), "lon": lax.axis_size("lon")}
    stages = stages_of(sizes)
    widest = max(members for _, _, members in stages)
    tile = jnp.zeros((8, 128), jnp.float32).at[0, : local.shape[0]].set(local)
    summed = pl.pallas_call(
        functools.partial(reduce_kernel, stages),
        out_shape=jax.ShapeDtypeStruct((8, 128), jnp.float32),
        in_specs=[pl.BlockSpec(memory_space=pltpu.VMEM)],
        out_specs=pl.BlockSpec(memory_space=pltpu.VMEM),
        scratch_shapes=[
            pltpu.VMEM((len(stages), 8, 128), jnp.float32),
            pltpu.VMEM((len(stages), widest, 8, 128), jnp.float32),
            pltpu.SemaphoreType.DMA((len(stages), widest)),
            pltpu.SemaphoreType.DMA((len(stages), widest)),
        ],
        compiler_params=pltpu.CompilerParams(collective_id=0, has_side_effects=True),
    )(tile)
    return summed[0, : local.shape[0]]


def interior(field):
    rows, cols = MARGIN_ROWS, MARGIN_COLS
    return field[..., : -2 * rows, : -2 * cols]


def sums(*pairs):
    local = jnp.stack([jnp.sum(interior(x) * interior(y)) for x, y in pairs])
    return all_sum(local)


def per_device(surface, bathymetry, land_sea, flux_lon, flux_lat):
    sea = land_sea.astype(jnp.float32)
    surface_x, bathymetry_x, sea_x, flux_lon_x, flux_lat_x = grow([surface, bathymetry, sea, flux_lon, flux_lat])
    wet = jnp.stack([sea_x * east(sea_x), sea_x * north(sea_x)])
    depth = jnp.stack([0.5 * (bathymetry_x + east(bathymetry_x)), 0.5 * (bathymetry_x + north(bathymetry_x))])
    slope = jnp.stack([east(surface_x) - surface_x, north(surface_x) - surface_x])
    start = wet * (jnp.stack([flux_lon_x, flux_lat_x]) - courant * depth * slope)
    inverse = jnp.where(depth > 0, 1.0 / (dispersion * depth * depth), 0.0)
    right_side = wet * inverse * start
    solution = start
    residual = right_side - operate(start, wet, inverse)
    applied = operate(residual, wet, inverse)
    norm_now, curve = sums((residual, residual), (residual, applied))
    direction, image = residual, applied
    for step in range(ITERS):
        alpha = norm_now / curve
        solution = solution + alpha * direction
        if step == ITERS - 1:
            break
        residual = residual - alpha * image
        applied = operate(residual, wet, inverse)
        norm_next, r_ar, r_ap = sums((residual, residual), (residual, applied), (residual, image))
        beta = norm_next / norm_now
        curve = r_ar + 2.0 * beta * r_ap + beta * beta * curve
        direction = residual + beta * direction
        image = applied + beta * image
        norm_now = norm_next
    surface_next = interior(surface_x - continuity * divergence(solution))
    solution = interior(solution)
    return (surface_next, solution[0], solution[1])


def solution(mesh):
    in_specs = (P("lat", "lon"), P("lat", "lon"), P("lat", "lon"), P("lat", "lon"), P("lat", "lon"))
    out_specs = (P("lat", "lon"), P("lat", "lon"), P("lat", "lon"))
    return jax.shard_map(
        per_device, mesh=mesh, in_specs=in_specs, out_specs=out_specs, check_vma=False
    )
```

```python
import functools

import jax
import jax.numpy as jnp
from jax import lax
from jax.experimental import pallas as pl
from jax.experimental.pallas import tpu as pltpu
from jax.sharding import PartitionSpec as P

MESH = pl.DeviceIdType.MESH

ITERS = 3
MARGIN_ROWS = 8
MARGIN_COLS = 8


courant = -0.4
dispersion = 40.0
continuity = -0.5


def from_behind(value, axis, steps):
    count = lax.axis_size(axis)
    leading, last = (max(0, -steps), min(count, count - steps))
    return lax.ppermute(value, axis, [(source, source + steps) for source in range(leading, last)])


def grow(stacked):
    rows, cols = MARGIN_ROWS, MARGIN_COLS
    above = from_behind(stacked[:, :rows, :], "lat", -1)
    below = from_behind(stacked[:, -rows:, :], "lat", 1)
    stacked = jnp.concatenate([below, stacked, above], axis=1)
    right = from_behind(stacked[:, :, :cols], "lon", -1)
    left = from_behind(stacked[:, :, -cols:], "lon", 1)
    return jnp.concatenate([left, stacked, right], axis=2)


def east(field):
    return jnp.pad(field[..., :, 1:], [(0, 0)] * (field.ndim - 1) + [(0, 1)])


def north(field):
    return jnp.pad(field[..., 1:, :], [(0, 0)] * (field.ndim - 2) + [(0, 1), (0, 0)])


def west(field):
    return jnp.pad(field[..., :, :-1], [(0, 0)] * (field.ndim - 1) + [(1, 0)])


def south(field):
    return jnp.pad(field[..., :-1, :], [(0, 0)] * (field.ndim - 2) + [(1, 0), (0, 0)])


def divergence(field):
    return field[0] - west(field[0]) + field[1] - south(field[1])


def operate(field, wet, inverse):
    diverge = divergence(field)
    back = jnp.stack([diverge - east(diverge), diverge - north(diverge)])
    return wet * (inverse * field + back)


def stages_of(sizes):
    return tuple((axis, 1, sizes[axis]) for axis in ("lon", "lat") if sizes[axis] > 1)


def reduce_kernel(stages, local_ref, out_ref, parts, got, send_sem, recv_sem):
    me = {"lat": lax.axis_index("lat"), "lon": lax.axis_index("lon")}

    def partner(axis, stride, members, offset):
        own = me[axis]
        digit = (own // stride) % members
        other = own - digit * stride + ((digit + offset) % members) * stride
        return tuple(other if name == axis else me[name] for name in ("lat", "lon"))

    value = local_ref[...]
    for stage, (axis, stride, members) in enumerate(stages):
        parts[stage] = value
        got[stage, 0] = value
        copies = []
        for offset in range(1, members):
            slot = members - offset
            copy = pltpu.make_async_remote_copy(
                src_ref=parts.at[stage],
                dst_ref=got.at[stage, slot],
                send_sem=send_sem.at[stage, offset],
                recv_sem=recv_sem.at[stage, slot],
                device_id=partner(axis, stride, members, offset),
                device_id_type=MESH,
            )
            copy.start()
            copies.append(copy)
        for copy in copies:
            copy.wait()
        digit = (me[axis] // stride) % members
        ordered = [got[stage, (member - digit) % members] for member in range(members)]
        while len(ordered) > 1:
            ordered = [ordered[k] + ordered[k + 1] for k in range(0, len(ordered), 2)]
        value = ordered[0]
    out_ref[...] = value


def all_sum(local):
    sizes = {"lat": lax.axis_size("lat"), "lon": lax.axis_size("lon")}
    stages = stages_of(sizes)
    widest = max(members for _, _, members in stages)
    tile = jnp.zeros((8, 128), jnp.float32).at[0, : local.shape[0]].set(local)
    summed = pl.pallas_call(
        functools.partial(reduce_kernel, stages),
        out_shape=jax.ShapeDtypeStruct((8, 128), jnp.float32),
        in_specs=[pl.BlockSpec(memory_space=pltpu.VMEM)],
        out_specs=pl.BlockSpec(memory_space=pltpu.VMEM),
        scratch_shapes=[
            pltpu.VMEM((len(stages), 8, 128), jnp.float32),
            pltpu.VMEM((len(stages), widest, 8, 128), jnp.float32),
            pltpu.SemaphoreType.DMA((len(stages), widest)),
            pltpu.SemaphoreType.DMA((len(stages), widest)),
        ],
        compiler_params=pltpu.CompilerParams(has_side_effects=True),
    )(tile)
    return summed[0, : local.shape[0]]


def interior(field):
    rows, cols = MARGIN_ROWS, MARGIN_COLS
    return field[..., rows:-rows, cols:-cols]


def sums(*pairs):
    local = jnp.stack([jnp.sum(interior(x) * interior(y)) for x, y in pairs])
    return all_sum(local)


def per_device(surface, bathymetry, land_sea, flux_lon, flux_lat):
    sea = land_sea.astype(jnp.float32)
    grown = grow(jnp.stack([surface, bathymetry, sea, flux_lon, flux_lat]))
    surface_x, bathymetry_x, sea_x = grown[0], grown[1], grown[2]
    wet = jnp.stack([sea_x * east(sea_x), sea_x * north(sea_x)])
    depth = jnp.stack([0.5 * (bathymetry_x + east(bathymetry_x)), 0.5 * (bathymetry_x + north(bathymetry_x))])
    slope = jnp.stack([east(surface_x) - surface_x, north(surface_x) - surface_x])
    start = wet * (grown[3:] - courant * depth * slope)
    inverse = jnp.where(depth > 0, 1.0 / (dispersion * depth * depth), 0.0)
    right_side = wet * inverse * start
    solution = start
    residual = right_side - operate(start, wet, inverse)
    applied = operate(residual, wet, inverse)
    norm_now, curve = sums((residual, residual), (residual, applied))
    direction, image = residual, applied
    for step in range(ITERS):
        alpha = norm_now / curve
        solution = solution + alpha * direction
        if step == ITERS - 1:
            break
        residual = residual - alpha * image
        applied = operate(residual, wet, inverse)
        norm_next, r_ar, r_ap = sums((residual, residual), (residual, applied), (residual, image))
        beta = norm_next / norm_now
        curve = r_ar + 2.0 * beta * r_ap + beta * beta * curve
        direction = residual + beta * direction
        image = applied + beta * image
        norm_now = norm_next
    surface_next = interior(surface_x - continuity * divergence(solution))
    solution = interior(solution)
    return (surface_next, solution[0], solution[1])


def solution(mesh):
    in_specs = (P("lat", "lon"), P("lat", "lon"), P("lat", "lon"), P("lat", "lon"), P("lat", "lon"))
    out_specs = (P("lat", "lon"), P("lat", "lon"), P("lat", "lon"))
    return jax.shard_map(
        per_device, mesh=mesh, in_specs=in_specs, out_specs=out_specs, check_vma=False
    )
```

```python
import functools

import jax
import jax.numpy as jnp
from jax import lax
from jax.experimental import pallas as pl
from jax.experimental.pallas import tpu as pltpu
from jax.sharding import PartitionSpec as P

MESH = pl.DeviceIdType.MESH

ITERS = 3
MARGIN_ROWS = 8
MARGIN_COLS = 8


courant = -0.4
dispersion = 40.0
continuity = -0.5


def from_behind(value, axis, steps):
    count = lax.axis_size(axis)
    leading, last = (max(0, -steps), min(count, count - steps))
    return lax.ppermute(value, axis, [(source, source + steps) for source in range(leading, last)])


def grow(stacked):
    rows, cols = MARGIN_ROWS, MARGIN_COLS
    above = from_behind(stacked[:, :rows, :], "lat", -1)
    below = from_behind(stacked[:, -rows:, :], "lat", 1)
    stacked = jnp.concatenate([below, stacked, above], axis=1)
    right = from_behind(stacked[:, :, :cols], "lon", -1)
    left = from_behind(stacked[:, :, -cols:], "lon", 1)
    return jnp.concatenate([left, stacked, right], axis=2)


def east(field):
    return jnp.pad(field[..., :, 1:], [(0, 0)] * (field.ndim - 1) + [(0, 1)])


def north(field):
    return jnp.pad(field[..., 1:, :], [(0, 0)] * (field.ndim - 2) + [(0, 1), (0, 0)])


def west(field):
    return jnp.pad(field[..., :, :-1], [(0, 0)] * (field.ndim - 1) + [(1, 0)])


def south(field):
    return jnp.pad(field[..., :-1, :], [(0, 0)] * (field.ndim - 2) + [(1, 0), (0, 0)])


def divergence(field):
    return field[0] - west(field[0]) + field[1] - south(field[1])


def operate(field, wet, inverse):
    diverge = divergence(field)
    back = jnp.stack([diverge - east(diverge), diverge - north(diverge)])
    return wet * (inverse * field + back)


def stages_of(sizes):
    return tuple((axis, 1, sizes[axis]) for axis in ("lon", "lat") if sizes[axis] > 1)


def reduce_kernel(stages, local_ref, prev_ref, out_ref, parts, got, send_sem, recv_sem):
    me = {"lat": lax.axis_index("lat"), "lon": lax.axis_index("lon")}

    def partner(axis, stride, members, offset):
        own = me[axis]
        digit = (own // stride) % members
        other = own - digit * stride + ((digit + offset) % members) * stride
        return tuple(other if name == axis else me[name] for name in ("lat", "lon"))

    barrier = pltpu.get_barrier_semaphore()
    greeted = 0
    for axis, stride, members in stages:
        for offset in range(1, members):
            pl.semaphore_signal(barrier, inc=1, device_id=partner(axis, stride, members, offset), device_id_type=MESH)
            greeted += 1
    pl.semaphore_wait(barrier, greeted)

    value = local_ref[...]
    for stage, (axis, stride, members) in enumerate(stages):
        parts[stage] = value
        got[stage, 0] = value
        copies = []
        for offset in range(1, members):
            slot = members - offset
            copy = pltpu.make_async_remote_copy(
                src_ref=parts.at[stage],
                dst_ref=got.at[stage, slot],
                send_sem=send_sem.at[stage, offset],
                recv_sem=recv_sem.at[stage, slot],
                device_id=partner(axis, stride, members, offset),
                device_id_type=MESH,
            )
            copy.start()
            copies.append(copy)
        for copy in copies:
            copy.wait()
        digit = (me[axis] // stride) % members
        ordered = [got[stage, (member - digit) % members] for member in range(members)]
        while len(ordered) > 1:
            ordered = [ordered[k] + ordered[k + 1] for k in range(0, len(ordered), 2)]
        value = ordered[0]
    norm, r_ar, r_ap = value[0:1], value[1:2], value[2:3]
    beta = norm / prev_ref[2:3]
    curve = r_ar + 2.0 * beta * r_ap + beta * beta * prev_ref[3:4]
    out_ref[...] = jnp.zeros_like(value)
    out_ref[0:1] = norm / curve
    out_ref[1:2] = beta
    out_ref[2:3] = norm
    out_ref[3:4] = curve


def cg_scalars(local, previous):
    sizes = {"lat": lax.axis_size("lat"), "lon": lax.axis_size("lon")}
    stages = stages_of(sizes)
    widest = max(members for _, _, members in stages)
    rows = lax.broadcasted_iota(jnp.int32, (8, 128), 0)
    tile = jnp.zeros((8, 128), jnp.float32)
    for k in range(local.shape[0]):
        tile = jnp.where(rows == k, local[k], tile)
    return pl.pallas_call(
        functools.partial(reduce_kernel, stages),
        out_shape=jax.ShapeDtypeStruct((8, 128), jnp.float32),
        in_specs=[pl.BlockSpec(memory_space=pltpu.VMEM)] * 2,
        out_specs=pl.BlockSpec(memory_space=pltpu.VMEM),
        scratch_shapes=[
            pltpu.VMEM((len(stages), 8, 128), jnp.float32),
            pltpu.VMEM((len(stages), widest, 8, 128), jnp.float32),
            pltpu.SemaphoreType.DMA((len(stages), widest)),
            pltpu.SemaphoreType.DMA((len(stages), widest)),
        ],
        compiler_params=pltpu.CompilerParams(collective_id=0, has_side_effects=True),
    )(tile, previous)


def interior(field):
    rows, cols = MARGIN_ROWS, MARGIN_COLS
    return field[..., rows:-rows, cols:-cols]


def dots(*pairs):
    return jnp.stack([jnp.sum(interior(x) * interior(y)) for x, y in pairs])


def per_device(surface, bathymetry, land_sea, flux_lon, flux_lat):
    sea = land_sea.astype(jnp.float32)
    grown = grow(jnp.stack([surface, bathymetry, sea, flux_lon, flux_lat]))
    surface_x, bathymetry_x, sea_x = grown[0], grown[1], grown[2]
    wet = jnp.stack([sea_x * east(sea_x), sea_x * north(sea_x)])
    depth = jnp.stack([0.5 * (bathymetry_x + east(bathymetry_x)), 0.5 * (bathymetry_x + north(bathymetry_x))])
    slope = jnp.stack([east(surface_x) - surface_x, north(surface_x) - surface_x])
    start = wet * (grown[3:] - courant * depth * slope)
    inverse = jnp.where(depth > 0, 1.0 / (dispersion * depth * depth), 0.0)
    right_side = wet * inverse * start
    solution = start
    residual = right_side - operate(start, wet, inverse)
    applied = operate(residual, wet, inverse)
    rows = lax.broadcasted_iota(jnp.int32, (8, 128), 0)
    previous = jnp.where(rows == 2, jnp.inf, 0.0).astype(jnp.float32)
    stats = cg_scalars(dots((residual, residual), (residual, applied)), previous)
    direction, image = residual, applied
    for step in range(ITERS):
        alpha = stats[0, 0]
        solution = solution + alpha * direction
        if step == ITERS - 1:
            break
        residual = residual - alpha * image
        applied = operate(residual, wet, inverse)
        stats = cg_scalars(dots((residual, residual), (residual, applied), (residual, image)), stats)
        beta = stats[1, 0]
        direction = residual + beta * direction
        image = applied + beta * image
    surface_next = interior(surface_x - continuity * divergence(solution))
    solution = interior(solution)
    return (surface_next, solution[0], solution[1])


def solution(mesh):
    in_specs = (P("lat", "lon"), P("lat", "lon"), P("lat", "lon"), P("lat", "lon"), P("lat", "lon"))
    out_specs = (P("lat", "lon"), P("lat", "lon"), P("lat", "lon"))
    return jax.shard_map(
        per_device, mesh=mesh, in_specs=in_specs, out_specs=out_specs, check_vma=False
    )
```

```python
import functools

import jax
import jax.numpy as jnp
from jax import lax
from jax.experimental import pallas as pl
from jax.experimental.pallas import tpu as pltpu
from jax.sharding import PartitionSpec as P

MESH = pl.DeviceIdType.MESH

ITERS = 3
MARGIN_ROWS = 8
MARGIN_COLS = 8


courant = -0.4
dispersion = 40.0
continuity = -0.5


def from_behind(value, axis, steps):
    count = lax.axis_size(axis)
    leading, last = (max(0, -steps), min(count, count - steps))
    return lax.ppermute(value, axis, [(source, source + steps) for source in range(leading, last)])


def from_corner(value, lat_steps, lon_steps):
    lats, lons = lax.axis_size("lat"), lax.axis_size("lon")
    pairs = [
        (lat * lons + lon, (lat + lat_steps) * lons + lon + lon_steps)
        for lat in range(lats)
        for lon in range(lons)
        if 0 <= lat + lat_steps < lats and 0 <= lon + lon_steps < lons
    ]
    return lax.ppermute(value, ("lat", "lon"), pairs)


def grow(stacked):
    rows, cols = MARGIN_ROWS, MARGIN_COLS
    above = from_behind(stacked[:, :rows, :], "lat", -1)
    below = from_behind(stacked[:, -rows:, :], "lat", 1)
    right = from_behind(stacked[:, :, :cols], "lon", -1)
    left = from_behind(stacked[:, :, -cols:], "lon", 1)
    north_east = from_corner(stacked[:, :rows, :cols], -1, -1)
    north_west = from_corner(stacked[:, :rows, -cols:], -1, 1)
    south_east = from_corner(stacked[:, -rows:, :cols], 1, -1)
    south_west = from_corner(stacked[:, -rows:, -cols:], 1, 1)
    return jnp.concatenate(
        [
            jnp.concatenate([south_west, below, south_east], axis=2),
            jnp.concatenate([left, stacked, right], axis=2),
            jnp.concatenate([north_west, above, north_east], axis=2),
        ],
        axis=1,
    )


def east(field):
    return jnp.pad(field[..., :, 1:], [(0, 0)] * (field.ndim - 1) + [(0, 1)])


def north(field):
    return jnp.pad(field[..., 1:, :], [(0, 0)] * (field.ndim - 2) + [(0, 1), (0, 0)])


def west(field):
    return jnp.pad(field[..., :, :-1], [(0, 0)] * (field.ndim - 1) + [(1, 0)])


def south(field):
    return jnp.pad(field[..., :-1, :], [(0, 0)] * (field.ndim - 2) + [(1, 0), (0, 0)])


def divergence(field):
    return field[0] - west(field[0]) + field[1] - south(field[1])


def operate(field, wet, inverse):
    diverge = divergence(field)
    back = jnp.stack([diverge - east(diverge), diverge - north(diverge)])
    return wet * (inverse * field + back)


def stages_of(sizes):
    return tuple((axis, 1, sizes[axis]) for axis in ("lon", "lat") if sizes[axis] > 1)


def reduce_kernel(stages, local_ref, prev_ref, out_ref, parts, got, send_sem, recv_sem):
    me = {"lat": lax.axis_index("lat"), "lon": lax.axis_index("lon")}

    def partner(axis, stride, members, offset):
        own = me[axis]
        digit = (own // stride) % members
        other = own - digit * stride + ((digit + offset) % members) * stride
        return tuple(other if name == axis else me[name] for name in ("lat", "lon"))

    barrier = pltpu.get_barrier_semaphore()
    greeted = 0
    for axis, stride, members in stages:
        for offset in range(1, members):
            pl.semaphore_signal(barrier, inc=1, device_id=partner(axis, stride, members, offset), device_id_type=MESH)
            greeted += 1
    pl.semaphore_wait(barrier, greeted)

    value = local_ref[...]
    for stage, (axis, stride, members) in enumerate(stages):
        parts[stage] = value
        got[stage, 0] = value
        copies = []
        for offset in range(1, members):
            slot = members - offset
            copy = pltpu.make_async_remote_copy(
                src_ref=parts.at[stage],
                dst_ref=got.at[stage, slot],
                send_sem=send_sem.at[stage, offset],
                recv_sem=recv_sem.at[stage, slot],
                device_id=partner(axis, stride, members, offset),
                device_id_type=MESH,
            )
            copy.start()
            copies.append(copy)
        for copy in copies:
            copy.wait()
        digit = (me[axis] // stride) % members
        ordered = [got[stage, (member - digit) % members] for member in range(members)]
        while len(ordered) > 1:
            ordered = [ordered[k] + ordered[k + 1] for k in range(0, len(ordered), 2)]
        value = ordered[0]
    norm, r_ar, r_ap = value[0:1], value[1:2], value[2:3]
    beta = norm / prev_ref[2:3]
    curve = r_ar + 2.0 * beta * r_ap + beta * beta * prev_ref[3:4]
    out_ref[...] = jnp.zeros_like(value)
    out_ref[0:1] = norm / curve
    out_ref[1:2] = beta
    out_ref[2:3] = norm
    out_ref[3:4] = curve


def cg_scalars(local, previous):
    sizes = {"lat": lax.axis_size("lat"), "lon": lax.axis_size("lon")}
    stages = stages_of(sizes)
    widest = max(members for _, _, members in stages)
    rows = lax.broadcasted_iota(jnp.int32, (8, 128), 0)
    tile = jnp.zeros((8, 128), jnp.float32)
    for k in range(local.shape[0]):
        tile = jnp.where(rows == k, local[k], tile)
    return pl.pallas_call(
        functools.partial(reduce_kernel, stages),
        out_shape=jax.ShapeDtypeStruct((8, 128), jnp.float32),
        in_specs=[pl.BlockSpec(memory_space=pltpu.VMEM)] * 2,
        out_specs=pl.BlockSpec(memory_space=pltpu.VMEM),
        scratch_shapes=[
            pltpu.VMEM((len(stages), 8, 128), jnp.float32),
            pltpu.VMEM((len(stages), widest, 8, 128), jnp.float32),
            pltpu.SemaphoreType.DMA((len(stages), widest)),
            pltpu.SemaphoreType.DMA((len(stages), widest)),
        ],
        compiler_params=pltpu.CompilerParams(collective_id=0, has_side_effects=True),
    )(tile, previous)


def interior(field):
    rows, cols = MARGIN_ROWS, MARGIN_COLS
    return field[..., rows:-rows, cols:-cols]


def dots(*pairs):
    return jnp.stack([jnp.sum(interior(x) * interior(y)) for x, y in pairs])


def per_device(surface, bathymetry, land_sea, flux_lon, flux_lat):
    sea = land_sea.astype(jnp.float32)
    grown = grow(jnp.stack([surface, bathymetry, sea, flux_lon, flux_lat]))
    surface_x, bathymetry_x, sea_x = grown[0], grown[1], grown[2]
    wet = jnp.stack([sea_x * east(sea_x), sea_x * north(sea_x)])
    depth = jnp.stack([0.5 * (bathymetry_x + east(bathymetry_x)), 0.5 * (bathymetry_x + north(bathymetry_x))])
    slope = jnp.stack([east(surface_x) - surface_x, north(surface_x) - surface_x])
    start = wet * (grown[3:] - courant * depth * slope)
    inverse = jnp.where(depth > 0, 1.0 / (dispersion * depth * depth), 0.0)
    right_side = wet * inverse * start
    solution = start
    residual = right_side - operate(start, wet, inverse)
    applied = operate(residual, wet, inverse)
    rows = lax.broadcasted_iota(jnp.int32, (8, 128), 0)
    previous = jnp.where(rows == 2, jnp.inf, 0.0).astype(jnp.float32)
    stats = cg_scalars(dots((residual, residual), (residual, applied)), previous)
    direction, image = residual, applied
    for step in range(ITERS):
        alpha = stats[0, 0]
        solution = solution + alpha * direction
        if step == ITERS - 1:
            break
        residual = residual - alpha * image
        applied = operate(residual, wet, inverse)
        stats = cg_scalars(dots((residual, residual), (residual, applied), (residual, image)), stats)
        beta = stats[1, 0]
        direction = residual + beta * direction
        image = applied + beta * image
    surface_next = interior(surface_x - continuity * divergence(solution))
    solution = interior(solution)
    return (surface_next, solution[0], solution[1])


def solution(mesh):
    in_specs = (P("lat", "lon"), P("lat", "lon"), P("lat", "lon"), P("lat", "lon"), P("lat", "lon"))
    out_specs = (P("lat", "lon"), P("lat", "lon"), P("lat", "lon"))
    return jax.shard_map(
        per_device, mesh=mesh, in_specs=in_specs, out_specs=out_specs, check_vma=False
    )
```

```python
import functools

import numpy as np

import jax
import jax.numpy as jnp
from jax import lax
from jax.experimental import pallas as pl
from jax.experimental.pallas import tpu as pltpu
from jax.sharding import PartitionSpec as P

MESH = pl.DeviceIdType.MESH

ITERS = 3
MARGIN_ROWS = 8
MARGIN_COLS = 8


courant = -0.4
dispersion = 40.0
continuity = -0.5


def from_behind(value, axis, steps):
    count = lax.axis_size(axis)
    leading, last = (max(0, -steps), min(count, count - steps))
    return lax.ppermute(value, axis, [(source, source + steps) for source in range(leading, last)])


def grow(stacked):
    rows, cols = MARGIN_ROWS, MARGIN_COLS
    above = from_behind(stacked[:, :rows, :], "lat", -1)
    below = from_behind(stacked[:, -rows:, :], "lat", 1)
    stacked = jnp.concatenate([below, stacked, above], axis=1)
    right = from_behind(stacked[:, :, :cols], "lon", -1)
    left = from_behind(stacked[:, :, -cols:], "lon", 1)
    return jnp.concatenate([left, stacked, right], axis=2)


def east(field):
    return jnp.pad(field[..., :, 1:], [(0, 0)] * (field.ndim - 1) + [(0, 1)])


def north(field):
    return jnp.pad(field[..., 1:, :], [(0, 0)] * (field.ndim - 2) + [(0, 1), (0, 0)])


def west(field):
    return jnp.pad(field[..., :, :-1], [(0, 0)] * (field.ndim - 1) + [(1, 0)])


def south(field):
    return jnp.pad(field[..., :-1, :], [(0, 0)] * (field.ndim - 2) + [(1, 0), (0, 0)])


def divergence(field):
    return field[0] - west(field[0]) + field[1] - south(field[1])


def gradient_back(field):
    diverge = divergence(field)
    return jnp.stack([diverge - east(diverge), diverge - north(diverge)])


def operate(field, wet, inverse):
    return wet * (inverse * field + gradient_back(field))


def stages_of(sizes):
    return tuple((axis, 1, sizes[axis]) for axis in ("lon", "lat") if sizes[axis] > 1)


def reduce_kernel(stages, local_ref, prev_ref, out_ref, parts, got, send_sem, recv_sem):
    me = {"lat": lax.axis_index("lat"), "lon": lax.axis_index("lon")}

    def partner(axis, stride, members, offset):
        own = me[axis]
        digit = (own // stride) % members
        other = own - digit * stride + ((digit + offset) % members) * stride
        return tuple(other if name == axis else me[name] for name in ("lat", "lon"))

    barrier = pltpu.get_barrier_semaphore()
    greeted = 0
    for axis, stride, members in stages:
        for offset in range(1, members):
            pl.semaphore_signal(barrier, inc=1, device_id=partner(axis, stride, members, offset), device_id_type=MESH)
            greeted += 1
    pl.semaphore_wait(barrier, greeted)

    value = local_ref[...]
    for stage, (axis, stride, members) in enumerate(stages):
        parts[stage] = value
        got[stage, 0] = value
        copies = []
        for offset in range(1, members):
            slot = members - offset
            copy = pltpu.make_async_remote_copy(
                src_ref=parts.at[stage],
                dst_ref=got.at[stage, slot],
                send_sem=send_sem.at[stage, offset],
                recv_sem=recv_sem.at[stage, slot],
                device_id=partner(axis, stride, members, offset),
                device_id_type=MESH,
            )
            copy.start()
            copies.append(copy)
        for copy in copies:
            copy.wait()
        digit = (me[axis] // stride) % members
        ordered = [got[stage, (member - digit) % members] for member in range(members)]
        while len(ordered) > 1:
            ordered = [ordered[k] + ordered[k + 1] for k in range(0, len(ordered), 2)]
        value = ordered[0]
    norm, r_ar, r_ap = value[0:1], value[1:2], value[2:3]
    beta = norm / prev_ref[2:3]
    curve = r_ar + 2.0 * beta * r_ap + beta * beta * prev_ref[3:4]
    out_ref[...] = jnp.zeros_like(value)
    out_ref[0:1] = norm / curve
    out_ref[1:2] = beta
    out_ref[2:3] = norm
    out_ref[3:4] = curve


def cg_scalars(local, previous):
    sizes = {"lat": lax.axis_size("lat"), "lon": lax.axis_size("lon")}
    stages = stages_of(sizes)
    widest = max(members for _, _, members in stages)
    rows = lax.broadcasted_iota(jnp.int32, (8, 128), 0)
    tile = jnp.zeros((8, 128), jnp.float32)
    for k in range(local.shape[0]):
        tile = jnp.where(rows == k, local[k], tile)
    return pl.pallas_call(
        functools.partial(reduce_kernel, stages),
        out_shape=jax.ShapeDtypeStruct((8, 128), jnp.float32),
        in_specs=[pl.BlockSpec(memory_space=pltpu.VMEM)] * 2,
        out_specs=pl.BlockSpec(memory_space=pltpu.VMEM),
        scratch_shapes=[
            pltpu.VMEM((len(stages), 8, 128), jnp.float32),
            pltpu.VMEM((len(stages), widest, 8, 128), jnp.float32),
            pltpu.SemaphoreType.DMA((len(stages), widest)),
            pltpu.SemaphoreType.DMA((len(stages), widest)),
        ],
        compiler_params=pltpu.CompilerParams(collective_id=0, has_side_effects=True),
    )(tile, previous)


def interior(field):
    rows, cols = MARGIN_ROWS, MARGIN_COLS
    return field[..., rows:-rows, cols:-cols]


def dots(*pairs):
    return jnp.stack([jnp.sum(interior(x) * interior(y)) for x, y in pairs])


def per_device(surface, bathymetry, land_sea, flux_lon, flux_lat):
    sea = land_sea.astype(jnp.float32)
    grown = grow(jnp.stack([surface, bathymetry, sea, flux_lon, flux_lat]))
    surface_x, bathymetry_x, sea_x = grown[0], grown[1], grown[2]
    eastern, northern = east(grown[:3]), north(grown[:3])
    wet = jnp.stack([sea_x * eastern[2], sea_x * northern[2]])
    depth = jnp.stack([0.5 * (bathymetry_x + eastern[1]), 0.5 * (bathymetry_x + northern[1])])
    slope = jnp.stack([eastern[0] - surface_x, northern[0] - surface_x])
    start = wet * (grown[3:] - courant * depth * slope)
    inverse = jnp.where(depth > 0, 1.0 / (dispersion * depth * depth), 0.0)
    solution = start
    residual = -(wet * gradient_back(start))
    applied = operate(residual, wet, inverse)
    previous = np.zeros((8, 128), np.float32)
    previous[2] = np.inf
    previous = jnp.asarray(previous)
    stats = cg_scalars(dots((residual, residual), (residual, applied)), previous)
    direction, image = residual, applied
    for step in range(ITERS):
        alpha = stats[0, 0]
        solution = solution + alpha * direction
        if step == ITERS - 1:
            break
        residual = residual - alpha * image
        applied = operate(residual, wet, inverse)
        stats = cg_scalars(dots((residual, residual), (residual, applied), (residual, image)), stats)
        beta = stats[1, 0]
        direction = residual + beta * direction
        image = applied + beta * image
    surface_next = interior(surface_x - continuity * divergence(solution))
    solution = interior(solution)
    return (surface_next, solution[0], solution[1])


def solution(mesh):
    in_specs = (P("lat", "lon"), P("lat", "lon"), P("lat", "lon"), P("lat", "lon"), P("lat", "lon"))
    out_specs = (P("lat", "lon"), P("lat", "lon"), P("lat", "lon"))
    return jax.shard_map(
        per_device, mesh=mesh, in_specs=in_specs, out_specs=out_specs, check_vma=False
    )
```

```python
import functools

import jax
import jax.numpy as jnp
from jax import lax
from jax.experimental import pallas as pl
from jax.experimental.pallas import tpu as pltpu
from jax.sharding import PartitionSpec as P

MESH = pl.DeviceIdType.MESH

ITERS = 3
MARGIN_ROWS = 8
MARGIN_COLS = 8


courant = -0.4
dispersion = 40.0
continuity = -0.5


def from_behind(value, axis, steps):
    count = lax.axis_size(axis)
    leading, last = (max(0, -steps), min(count, count - steps))
    return lax.ppermute(value, axis, [(source, source + steps) for source in range(leading, last)])


def grow(stacked):
    rows, cols = MARGIN_ROWS, MARGIN_COLS
    above = from_behind(stacked[:, :rows, :], "lat", -1)
    below = from_behind(stacked[:, -rows:, :], "lat", 1)
    stacked = jnp.concatenate([below, stacked, above], axis=1)
    right = from_behind(stacked[:, :, :cols], "lon", -1)
    left = from_behind(stacked[:, :, -cols:], "lon", 1)
    return jnp.concatenate([stacked, right, left], axis=2)


def east(field):
    return jnp.roll(field, -1, axis=-1)


def north(field):
    return jnp.pad(field[..., 1:, :], [(0, 0)] * (field.ndim - 2) + [(0, 1), (0, 0)])


def west(field):
    return jnp.roll(field, 1, axis=-1)


def south(field):
    return jnp.pad(field[..., :-1, :], [(0, 0)] * (field.ndim - 2) + [(1, 0), (0, 0)])


def divergence(field):
    return field[0] - west(field[0]) + field[1] - south(field[1])


def operate(field, wet, inverse):
    diverge = divergence(field)
    back = jnp.stack([diverge - east(diverge), diverge - north(diverge)])
    return wet * (inverse * field + back)


def stages_of(sizes):
    return tuple((axis, 1, sizes[axis]) for axis in ("lon", "lat") if sizes[axis] > 1)


def reduce_kernel(stages, local_ref, prev_ref, out_ref, parts, got, send_sem, recv_sem):
    me = {"lat": lax.axis_index("lat"), "lon": lax.axis_index("lon")}

    def partner(axis, stride, members, offset):
        own = me[axis]
        digit = (own // stride) % members
        other = own - digit * stride + ((digit + offset) % members) * stride
        return tuple(other if name == axis else me[name] for name in ("lat", "lon"))

    barrier = pltpu.get_barrier_semaphore()
    greeted = 0
    for axis, stride, members in stages:
        for offset in range(1, members):
            pl.semaphore_signal(barrier, inc=1, device_id=partner(axis, stride, members, offset), device_id_type=MESH)
            greeted += 1
    pl.semaphore_wait(barrier, greeted)

    value = local_ref[...]
    for stage, (axis, stride, members) in enumerate(stages):
        parts[stage] = value
        got[stage, 0] = value
        copies = []
        for offset in range(1, members):
            slot = members - offset
            copy = pltpu.make_async_remote_copy(
                src_ref=parts.at[stage],
                dst_ref=got.at[stage, slot],
                send_sem=send_sem.at[stage, offset],
                recv_sem=recv_sem.at[stage, slot],
                device_id=partner(axis, stride, members, offset),
                device_id_type=MESH,
            )
            copy.start()
            copies.append(copy)
        for copy in copies:
            copy.wait()
        digit = (me[axis] // stride) % members
        ordered = [got[stage, (member - digit) % members] for member in range(members)]
        while len(ordered) > 1:
            ordered = [ordered[k] + ordered[k + 1] for k in range(0, len(ordered), 2)]
        value = ordered[0]
    norm, r_ar, r_ap = value[0:1], value[1:2], value[2:3]
    beta = norm / prev_ref[2:3]
    curve = r_ar + 2.0 * beta * r_ap + beta * beta * prev_ref[3:4]
    out_ref[...] = jnp.zeros_like(value)
    out_ref[0:1] = norm / curve
    out_ref[1:2] = beta
    out_ref[2:3] = norm
    out_ref[3:4] = curve


def cg_scalars(local, previous):
    sizes = {"lat": lax.axis_size("lat"), "lon": lax.axis_size("lon")}
    stages = stages_of(sizes)
    widest = max(members for _, _, members in stages)
    rows = lax.broadcasted_iota(jnp.int32, (8, 128), 0)
    tile = jnp.zeros((8, 128), jnp.float32)
    for k in range(local.shape[0]):
        tile = jnp.where(rows == k, local[k], tile)
    return pl.pallas_call(
        functools.partial(reduce_kernel, stages),
        out_shape=jax.ShapeDtypeStruct((8, 128), jnp.float32),
        in_specs=[pl.BlockSpec(memory_space=pltpu.VMEM)] * 2,
        out_specs=pl.BlockSpec(memory_space=pltpu.VMEM),
        scratch_shapes=[
            pltpu.VMEM((len(stages), 8, 128), jnp.float32),
            pltpu.VMEM((len(stages), widest, 8, 128), jnp.float32),
            pltpu.SemaphoreType.DMA((len(stages), widest)),
            pltpu.SemaphoreType.DMA((len(stages), widest)),
        ],
        compiler_params=pltpu.CompilerParams(collective_id=0, has_side_effects=True),
    )(tile, previous)


def interior(field):
    rows, cols = MARGIN_ROWS, MARGIN_COLS
    return field[..., rows:-rows, : -2 * cols]


def dots(*pairs):
    return jnp.stack([jnp.sum(interior(x) * interior(y)) for x, y in pairs])


def per_device(surface, bathymetry, land_sea, flux_lon, flux_lat):
    sea = land_sea.astype(jnp.float32)
    grown = grow(jnp.stack([surface, bathymetry, sea, flux_lon, flux_lat]))
    surface_x, bathymetry_x, sea_x = grown[0], grown[1], grown[2]
    wet = jnp.stack([sea_x * east(sea_x), sea_x * north(sea_x)])
    depth = jnp.stack([0.5 * (bathymetry_x + east(bathymetry_x)), 0.5 * (bathymetry_x + north(bathymetry_x))])
    slope = jnp.stack([east(surface_x) - surface_x, north(surface_x) - surface_x])
    start = wet * (grown[3:] - courant * depth * slope)
    inverse = jnp.where(depth > 0, 1.0 / (dispersion * depth * depth), 0.0)
    right_side = wet * inverse * start
    solution = start
    residual = right_side - operate(start, wet, inverse)
    applied = operate(residual, wet, inverse)
    rows = lax.broadcasted_iota(jnp.int32, (8, 128), 0)
    previous = jnp.where(rows == 2, jnp.inf, 0.0).astype(jnp.float32)
    stats = cg_scalars(dots((residual, residual), (residual, applied)), previous)
    direction, image = residual, applied
    for step in range(ITERS):
        alpha = stats[0, 0]
        solution = solution + alpha * direction
        if step == ITERS - 1:
            break
        residual = residual - alpha * image
        applied = operate(residual, wet, inverse)
        stats = cg_scalars(dots((residual, residual), (residual, applied), (residual, image)), stats)
        beta = stats[1, 0]
        direction = residual + beta * direction
        image = applied + beta * image
    surface_next = interior(surface_x - continuity * divergence(solution))
    solution = interior(solution)
    return (surface_next, solution[0], solution[1])


def solution(mesh):
    in_specs = (P("lat", "lon"), P("lat", "lon"), P("lat", "lon"), P("lat", "lon"), P("lat", "lon"))
    out_specs = (P("lat", "lon"), P("lat", "lon"), P("lat", "lon"))
    return jax.shard_map(
        per_device, mesh=mesh, in_specs=in_specs, out_specs=out_specs, check_vma=False
    )
```

```python
import functools

import jax
import jax.numpy as jnp
from jax import lax
from jax.experimental import pallas as pl
from jax.experimental.pallas import tpu as pltpu
from jax.sharding import PartitionSpec as P

MESH = pl.DeviceIdType.MESH

ITERS = 3
MARGIN_ROWS = 8
MARGIN_COLS = 8


courant = -0.4
dispersion = 40.0
continuity = -0.5


def from_behind(value, axis, steps):
    count = lax.axis_size(axis)
    leading, last = (max(0, -steps), min(count, count - steps))
    return lax.ppermute(value, axis, [(source, source + steps) for source in range(leading, last)])


def grow(stacked):
    rows, cols = MARGIN_ROWS, MARGIN_COLS
    above = from_behind(stacked[:, :rows, :], "lat", -1)
    below = from_behind(stacked[:, -rows:, :], "lat", 1)
    width = stacked.shape[2]
    wide = lax.optimization_barrier(jnp.pad(jnp.concatenate([below, stacked, above], axis=1), ((0, 0), (0, 0), (0, 2 * cols))))
    right = from_behind(wide[:, :, :cols], "lon", -1)
    left = from_behind(wide[:, :, width - cols : width], "lon", 1)
    return lax.dynamic_update_slice(wide, jnp.concatenate([right, left], axis=2), (0, 0, width))


def east(field):
    return jnp.roll(field, -1, axis=-1)


def north(field):
    return jnp.pad(field[..., 1:, :], [(0, 0)] * (field.ndim - 2) + [(0, 1), (0, 0)])


def west(field):
    return jnp.roll(field, 1, axis=-1)


def south(field):
    return jnp.pad(field[..., :-1, :], [(0, 0)] * (field.ndim - 2) + [(1, 0), (0, 0)])


def divergence(field):
    return field[0] - west(field[0]) + field[1] - south(field[1])


def operate(field, wet, inverse):
    diverge = divergence(field)
    back = jnp.stack([diverge - east(diverge), diverge - north(diverge)])
    return wet * (inverse * field + back)


def stages_of(sizes):
    return tuple((axis, 1, sizes[axis]) for axis in ("lon", "lat") if sizes[axis] > 1)


def reduce_kernel(stages, local_ref, prev_ref, out_ref, parts, got, send_sem, recv_sem):
    me = {"lat": lax.axis_index("lat"), "lon": lax.axis_index("lon")}

    def partner(axis, stride, members, offset):
        own = me[axis]
        digit = (own // stride) % members
        other = own - digit * stride + ((digit + offset) % members) * stride
        return tuple(other if name == axis else me[name] for name in ("lat", "lon"))

    barrier = pltpu.get_barrier_semaphore()
    greeted = 0
    for axis, stride, members in stages:
        for offset in range(1, members):
            pl.semaphore_signal(barrier, inc=1, device_id=partner(axis, stride, members, offset), device_id_type=MESH)
            greeted += 1
    pl.semaphore_wait(barrier, greeted)

    value = local_ref[...]
    for stage, (axis, stride, members) in enumerate(stages):
        parts[stage] = value
        got[stage, 0] = value
        copies = []
        for offset in range(1, members):
            slot = members - offset
            copy = pltpu.make_async_remote_copy(
                src_ref=parts.at[stage],
                dst_ref=got.at[stage, slot],
                send_sem=send_sem.at[stage, offset],
                recv_sem=recv_sem.at[stage, slot],
                device_id=partner(axis, stride, members, offset),
                device_id_type=MESH,
            )
            copy.start()
            copies.append(copy)
        for copy in copies:
            copy.wait()
        digit = (me[axis] // stride) % members
        ordered = [got[stage, (member - digit) % members] for member in range(members)]
        while len(ordered) > 1:
            ordered = [ordered[k] + ordered[k + 1] for k in range(0, len(ordered), 2)]
        value = ordered[0]
    norm, r_ar, r_ap = value[0:1], value[1:2], value[2:3]
    beta = norm / prev_ref[2:3]
    curve = r_ar + 2.0 * beta * r_ap + beta * beta * prev_ref[3:4]
    out_ref[...] = jnp.zeros_like(value)
    out_ref[0:1] = norm / curve
    out_ref[1:2] = beta
    out_ref[2:3] = norm
    out_ref[3:4] = curve


def cg_scalars(local, previous):
    sizes = {"lat": lax.axis_size("lat"), "lon": lax.axis_size("lon")}
    stages = stages_of(sizes)
    widest = max(members for _, _, members in stages)
    rows = lax.broadcasted_iota(jnp.int32, (8, 128), 0)
    tile = jnp.zeros((8, 128), jnp.float32)
    for k in range(local.shape[0]):
        tile = jnp.where(rows == k, local[k], tile)
    return pl.pallas_call(
        functools.partial(reduce_kernel, stages),
        out_shape=jax.ShapeDtypeStruct((8, 128), jnp.float32),
        in_specs=[pl.BlockSpec(memory_space=pltpu.VMEM)] * 2,
        out_specs=pl.BlockSpec(memory_space=pltpu.VMEM),
        scratch_shapes=[
            pltpu.VMEM((len(stages), 8, 128), jnp.float32),
            pltpu.VMEM((len(stages), widest, 8, 128), jnp.float32),
            pltpu.SemaphoreType.DMA((len(stages), widest)),
            pltpu.SemaphoreType.DMA((len(stages), widest)),
        ],
        compiler_params=pltpu.CompilerParams(collective_id=0, has_side_effects=True),
    )(tile, previous)


def interior(field):
    rows, cols = MARGIN_ROWS, MARGIN_COLS
    return field[..., rows:-rows, : -2 * cols]


def dots(*pairs):
    return jnp.stack([jnp.sum(interior(x) * interior(y)) for x, y in pairs])


def per_device(surface, bathymetry, land_sea, flux_lon, flux_lat):
    sea = land_sea.astype(jnp.float32)
    grown = grow(jnp.stack([surface, bathymetry, sea, flux_lon, flux_lat]))
    surface_x, bathymetry_x, sea_x = grown[0], grown[1], grown[2]
    wet = jnp.stack([sea_x * east(sea_x), sea_x * north(sea_x)])
    depth = jnp.stack([0.5 * (bathymetry_x + east(bathymetry_x)), 0.5 * (bathymetry_x + north(bathymetry_x))])
    slope = jnp.stack([east(surface_x) - surface_x, north(surface_x) - surface_x])
    start = wet * (grown[3:] - courant * depth * slope)
    inverse = jnp.where(depth > 0, 1.0 / (dispersion * depth * depth), 0.0)
    right_side = wet * inverse * start
    solution = start
    residual = right_side - operate(start, wet, inverse)
    applied = operate(residual, wet, inverse)
    rows = lax.broadcasted_iota(jnp.int32, (8, 128), 0)
    previous = jnp.where(rows == 2, jnp.inf, 0.0).astype(jnp.float32)
    stats = cg_scalars(dots((residual, residual), (residual, applied)), previous)
    direction, image = residual, applied
    for step in range(ITERS):
        alpha = stats[0, 0]
        solution = solution + alpha * direction
        if step == ITERS - 1:
            break
        residual = residual - alpha * image
        applied = operate(residual, wet, inverse)
        stats = cg_scalars(dots((residual, residual), (residual, applied), (residual, image)), stats)
        beta = stats[1, 0]
        direction = residual + beta * direction
        image = applied + beta * image
    surface_next = interior(surface_x - continuity * divergence(solution))
    solution = interior(solution)
    return (surface_next, solution[0], solution[1])


def solution(mesh):
    in_specs = (P("lat", "lon"), P("lat", "lon"), P("lat", "lon"), P("lat", "lon"), P("lat", "lon"))
    out_specs = (P("lat", "lon"), P("lat", "lon"), P("lat", "lon"))
    return jax.shard_map(
        per_device, mesh=mesh, in_specs=in_specs, out_specs=out_specs, check_vma=False
    )
```

```python
import functools

import jax
import jax.numpy as jnp
from jax import lax
from jax.experimental import pallas as pl
from jax.experimental.pallas import tpu as pltpu
from jax.sharding import PartitionSpec as P

MESH = pl.DeviceIdType.MESH

ITERS = 3
MARGIN_ROWS = 8
MARGIN_COLS = 8


courant = -0.4
dispersion = 40.0
continuity = -0.5


def from_behind(value, axis, steps):
    count = lax.axis_size(axis)
    leading, last = (max(0, -steps), min(count, count - steps))
    return lax.ppermute(value, axis, [(source, source + steps) for source in range(leading, last)])


def grow(stacked):
    rows, cols = MARGIN_ROWS, MARGIN_COLS
    above = from_behind(stacked[:, :rows, :], "lat", -1)
    below = from_behind(stacked[:, -rows:, :], "lat", 1)
    width = stacked.shape[2]
    wide = lax.optimization_barrier(jnp.pad(jnp.concatenate([below, stacked, above], axis=1), ((0, 0), (0, 0), (0, 2 * cols))))
    right = from_behind(wide[:, :, :cols], "lon", -1)
    left = from_behind(wide[:, :, width - cols : width], "lon", 1)
    return lax.dynamic_update_slice(wide, jnp.concatenate([right, left], axis=2), (0, 0, width))


def east(field):
    return jnp.roll(field, -1, axis=-1)


def north(field):
    return jnp.pad(field[..., 1:, :], [(0, 0)] * (field.ndim - 2) + [(0, 1), (0, 0)])


def west(field):
    return jnp.roll(field, 1, axis=-1)


def south(field):
    return jnp.pad(field[..., :-1, :], [(0, 0)] * (field.ndim - 2) + [(1, 0), (0, 0)])


def divergence(field):
    return field[0] - west(field[0]) + field[1] - south(field[1])


def operate(field, wet, inverse):
    diverge = divergence(field)
    back = jnp.stack([diverge - east(diverge), diverge - north(diverge)])
    return wet * (inverse * field + back)


def stages_of(sizes):
    return tuple((axis, 1, sizes[axis]) for axis in ("lon", "lat") if sizes[axis] > 1)


def reduce_kernel(stages, count, *refs):
    partial_refs, (prev_ref, out_ref, parts, got, send_sem, recv_sem) = refs[:count], refs[count:]
    me = {"lat": lax.axis_index("lat"), "lon": lax.axis_index("lon")}

    def partner(axis, stride, members, offset):
        own = me[axis]
        digit = (own // stride) % members
        other = own - digit * stride + ((digit + offset) % members) * stride
        return tuple(other if name == axis else me[name] for name in ("lat", "lon"))

    barrier = pltpu.get_barrier_semaphore()
    greeted = 0
    for axis, stride, members in stages:
        for offset in range(1, members):
            pl.semaphore_signal(barrier, inc=1, device_id=partner(axis, stride, members, offset), device_id_type=MESH)
            greeted += 1
    pl.semaphore_wait(barrier, greeted)

    rows = lax.broadcasted_iota(jnp.int32, (8, 128), 0)
    value = jnp.zeros((8, 128), jnp.float32)
    for k, partial_ref in enumerate(partial_refs):
        total = jnp.sum(jnp.sum(partial_ref[...], axis=1, keepdims=True), axis=0, keepdims=True)
        value = jnp.where(rows == k, total, value)
    for stage, (axis, stride, members) in enumerate(stages):
        parts[stage] = value
        got[stage, 0] = value
        copies = []
        for offset in range(1, members):
            slot = members - offset
            copy = pltpu.make_async_remote_copy(
                src_ref=parts.at[stage],
                dst_ref=got.at[stage, slot],
                send_sem=send_sem.at[stage, offset],
                recv_sem=recv_sem.at[stage, slot],
                device_id=partner(axis, stride, members, offset),
                device_id_type=MESH,
            )
            copy.start()
            copies.append(copy)
        for copy in copies:
            copy.wait()
        digit = (me[axis] // stride) % members
        ordered = [got[stage, (member - digit) % members] for member in range(members)]
        while len(ordered) > 1:
            ordered = [ordered[k] + ordered[k + 1] for k in range(0, len(ordered), 2)]
        value = ordered[0]
    norm, r_ar, r_ap = value[0:1], value[1:2], value[2:3]
    beta = norm / prev_ref[2:3]
    curve = r_ar + 2.0 * beta * r_ap + beta * beta * prev_ref[3:4]
    out_ref[...] = jnp.zeros_like(value)
    out_ref[0:1] = norm / curve
    out_ref[1:2] = beta
    out_ref[2:3] = norm
    out_ref[3:4] = curve


def cg_scalars(partials, previous):
    sizes = {"lat": lax.axis_size("lat"), "lon": lax.axis_size("lon")}
    stages = stages_of(sizes)
    widest = max(members for _, _, members in stages)
    return pl.pallas_call(
        functools.partial(reduce_kernel, stages, len(partials)),
        out_shape=jax.ShapeDtypeStruct((8, 128), jnp.float32),
        in_specs=[pl.BlockSpec(memory_space=pltpu.VMEM)] * (len(partials) + 1),
        out_specs=pl.BlockSpec(memory_space=pltpu.VMEM),
        scratch_shapes=[
            pltpu.VMEM((len(stages), 8, 128), jnp.float32),
            pltpu.VMEM((len(stages), widest, 8, 128), jnp.float32),
            pltpu.SemaphoreType.DMA((len(stages), widest)),
            pltpu.SemaphoreType.DMA((len(stages), widest)),
        ],
        compiler_params=pltpu.CompilerParams(collective_id=0, has_side_effects=True),
    )(*partials, previous)


def interior(field):
    rows, cols = MARGIN_ROWS, MARGIN_COLS
    return field[..., rows:-rows, : -2 * cols]


def dots(*pairs):
    def fold(x, y):
        product = interior(x) * interior(y)
        return jnp.sum(product.reshape(-1, 8, product.shape[-1] // 128, 128), axis=(0, 2))

    return [fold(x, y) for x, y in pairs]


def per_device(surface, bathymetry, land_sea, flux_lon, flux_lat):
    sea = land_sea.astype(jnp.float32)
    grown = grow(jnp.stack([surface, bathymetry, sea, flux_lon, flux_lat]))
    surface_x, bathymetry_x, sea_x = grown[0], grown[1], grown[2]
    wet = jnp.stack([sea_x * east(sea_x), sea_x * north(sea_x)])
    depth = jnp.stack([0.5 * (bathymetry_x + east(bathymetry_x)), 0.5 * (bathymetry_x + north(bathymetry_x))])
    slope = jnp.stack([east(surface_x) - surface_x, north(surface_x) - surface_x])
    start = wet * (grown[3:] - courant * depth * slope)
    inverse = jnp.where(depth > 0, 1.0 / (dispersion * depth * depth), 0.0)
    right_side = wet * inverse * start
    solution = start
    residual = right_side - operate(start, wet, inverse)
    applied = operate(residual, wet, inverse)
    rows = lax.broadcasted_iota(jnp.int32, (8, 128), 0)
    previous = jnp.where(rows == 2, jnp.inf, 0.0).astype(jnp.float32)
    stats = cg_scalars(dots((residual, residual), (residual, applied)) + [jnp.zeros((8, 128), jnp.float32)], previous)
    direction, image = residual, applied
    for step in range(ITERS):
        alpha = stats[0, 0]
        solution = solution + alpha * direction
        if step == ITERS - 1:
            break
        residual = residual - alpha * image
        applied = operate(residual, wet, inverse)
        stats = cg_scalars(dots((residual, residual), (residual, applied), (residual, image)), stats)
        beta = stats[1, 0]
        direction = residual + beta * direction
        image = applied + beta * image
    surface_next = interior(surface_x - continuity * divergence(solution))
    solution = interior(solution)
    return (surface_next, solution[0], solution[1])


def solution(mesh):
    in_specs = (P("lat", "lon"), P("lat", "lon"), P("lat", "lon"), P("lat", "lon"), P("lat", "lon"))
    out_specs = (P("lat", "lon"), P("lat", "lon"), P("lat", "lon"))
    return jax.shard_map(
        per_device, mesh=mesh, in_specs=in_specs, out_specs=out_specs, check_vma=False
    )
```

```python
import functools

import jax
import jax.numpy as jnp
from jax import lax
from jax.experimental import pallas as pl
from jax.experimental.pallas import tpu as pltpu
from jax.sharding import PartitionSpec as P

MESH = pl.DeviceIdType.MESH

ITERS = 3
MARGIN_ROWS = 8
MARGIN_COLS = 8
SENT = 4


courant = -0.4
dispersion = 40.0
continuity = -0.5


def from_behind(value, axis, steps):
    count = lax.axis_size(axis)
    leading, last = (max(0, -steps), min(count, count - steps))
    return lax.ppermute(value, axis, [(source, source + steps) for source in range(leading, last)])


def grow(stacked):
    rows, cols = MARGIN_ROWS, MARGIN_COLS
    above = from_behind(stacked[:, :rows, :], "lat", -1)
    below = from_behind(stacked[:, -rows:, :], "lat", 1)
    width = stacked.shape[2]
    wide = lax.optimization_barrier(jnp.pad(jnp.concatenate([below, stacked, above], axis=1), ((0, 0), (0, 0), (0, 2 * cols))))
    right = from_behind(wide[:, :, :cols], "lon", -1)
    left = from_behind(wide[:, :, width - cols : width], "lon", 1)
    return lax.dynamic_update_slice(wide, jnp.concatenate([right, left], axis=2), (0, 0, width))


def east(field):
    return jnp.roll(field, -1, axis=-1)


def north(field):
    return jnp.pad(field[..., 1:, :], [(0, 0)] * (field.ndim - 2) + [(0, 1), (0, 0)])


def west(field):
    return jnp.roll(field, 1, axis=-1)


def south(field):
    return jnp.pad(field[..., :-1, :], [(0, 0)] * (field.ndim - 2) + [(1, 0), (0, 0)])


def divergence(field):
    return field[0] - west(field[0]) + field[1] - south(field[1])


def operate(field, wet, inverse):
    diverge = divergence(field)
    back = jnp.stack([diverge - east(diverge), diverge - north(diverge)])
    return wet * (inverse * field + back)


def stages_of(sizes):
    return tuple((axis, 1, sizes[axis]) for axis in ("lon", "lat") if sizes[axis] > 1)


def reduce_kernel(stages, local_ref, prev_ref, out_ref, parts, got, send_sem, recv_sem):
    me = {"lat": lax.axis_index("lat"), "lon": lax.axis_index("lon")}

    def partner(axis, stride, members, offset):
        own = me[axis]
        digit = (own // stride) % members
        other = own - digit * stride + ((digit + offset) % members) * stride
        return tuple(other if name == axis else me[name] for name in ("lat", "lon"))

    barrier = pltpu.get_barrier_semaphore()
    greeted = 0
    for axis, stride, members in stages:
        for offset in range(1, members):
            pl.semaphore_signal(barrier, inc=1, device_id=partner(axis, stride, members, offset), device_id_type=MESH)
            greeted += 1
    pl.semaphore_wait(barrier, greeted)

    value = local_ref[0:SENT]
    for stage, (axis, stride, members) in enumerate(stages):
        parts[stage, 0:SENT] = value
        got[stage, 0, 0:SENT] = value
        copies = []
        for offset in range(1, members):
            slot = members - offset
            copy = pltpu.make_async_remote_copy(
                src_ref=parts.at[stage, pl.ds(0, SENT)],
                dst_ref=got.at[stage, slot, pl.ds(0, SENT)],
                send_sem=send_sem.at[stage, offset],
                recv_sem=recv_sem.at[stage, slot],
                device_id=partner(axis, stride, members, offset),
                device_id_type=MESH,
            )
            copy.start()
            copies.append(copy)
        for copy in copies:
            copy.wait()
        digit = (me[axis] // stride) % members
        ordered = [got[stage, (member - digit) % members, 0:SENT] for member in range(members)]
        while len(ordered) > 1:
            ordered = [ordered[k] + ordered[k + 1] for k in range(0, len(ordered), 2)]
        value = ordered[0]
    norm, r_ar, r_ap = value[0:1], value[1:2], value[2:3]
    beta = norm / prev_ref[2:3]
    curve = r_ar + 2.0 * beta * r_ap + beta * beta * prev_ref[3:4]
    out_ref[...] = jnp.zeros(out_ref.shape, out_ref.dtype)
    out_ref[0:1] = norm / curve
    out_ref[1:2] = beta
    out_ref[2:3] = norm
    out_ref[3:4] = curve


def cg_scalars(local, previous):
    sizes = {"lat": lax.axis_size("lat"), "lon": lax.axis_size("lon")}
    stages = stages_of(sizes)
    widest = max(members for _, _, members in stages)
    rows = lax.broadcasted_iota(jnp.int32, (8, 128), 0)
    tile = jnp.zeros((8, 128), jnp.float32)
    for k in range(local.shape[0]):
        tile = jnp.where(rows == k, local[k], tile)
    return pl.pallas_call(
        functools.partial(reduce_kernel, stages),
        out_shape=jax.ShapeDtypeStruct((8, 128), jnp.float32),
        in_specs=[pl.BlockSpec(memory_space=pltpu.VMEM)] * 2,
        out_specs=pl.BlockSpec(memory_space=pltpu.VMEM),
        scratch_shapes=[
            pltpu.VMEM((len(stages), 8, 128), jnp.float32),
            pltpu.VMEM((len(stages), widest, 8, 128), jnp.float32),
            pltpu.SemaphoreType.DMA((len(stages), widest)),
            pltpu.SemaphoreType.DMA((len(stages), widest)),
        ],
        compiler_params=pltpu.CompilerParams(collective_id=0, has_side_effects=True),
    )(tile, previous)


def interior(field):
    rows, cols = MARGIN_ROWS, MARGIN_COLS
    return field[..., rows:-rows, : -2 * cols]


def dots(*pairs):
    return jnp.stack([jnp.sum(interior(x) * interior(y)) for x, y in pairs])


def per_device(surface, bathymetry, land_sea, flux_lon, flux_lat):
    sea = land_sea.astype(jnp.float32)
    grown = grow(jnp.stack([surface, bathymetry, sea, flux_lon, flux_lat]))
    surface_x, bathymetry_x, sea_x = grown[0], grown[1], grown[2]
    wet = jnp.stack([sea_x * east(sea_x), sea_x * north(sea_x)])
    depth = jnp.stack([0.5 * (bathymetry_x + east(bathymetry_x)), 0.5 * (bathymetry_x + north(bathymetry_x))])
    slope = jnp.stack([east(surface_x) - surface_x, north(surface_x) - surface_x])
    start = wet * (grown[3:] - courant * depth * slope)
    inverse = jnp.where(depth > 0, 1.0 / (dispersion * depth * depth), 0.0)
    right_side = wet * inverse * start
    solution = start
    residual = right_side - operate(start, wet, inverse)
    applied = operate(residual, wet, inverse)
    rows = lax.broadcasted_iota(jnp.int32, (8, 128), 0)
    previous = jnp.where(rows == 2, jnp.inf, 0.0).astype(jnp.float32)
    stats = cg_scalars(dots((residual, residual), (residual, applied)), previous)
    direction, image = residual, applied
    for step in range(ITERS):
        alpha = stats[0, 0]
        solution = solution + alpha * direction
        if step == ITERS - 1:
            break
        residual = residual - alpha * image
        applied = operate(residual, wet, inverse)
        stats = cg_scalars(dots((residual, residual), (residual, applied), (residual, image)), stats)
        beta = stats[1, 0]
        direction = residual + beta * direction
        image = applied + beta * image
    surface_next = interior(surface_x - continuity * divergence(solution))
    solution = interior(solution)
    return (surface_next, solution[0], solution[1])


def solution(mesh):
    in_specs = (P("lat", "lon"), P("lat", "lon"), P("lat", "lon"), P("lat", "lon"), P("lat", "lon"))
    out_specs = (P("lat", "lon"), P("lat", "lon"), P("lat", "lon"))
    return jax.shard_map(
        per_device, mesh=mesh, in_specs=in_specs, out_specs=out_specs, check_vma=False
    )
```

```python
import functools

import jax
import jax.numpy as jnp
from jax import lax
from jax.experimental import pallas as pl
from jax.experimental.pallas import tpu as pltpu
from jax.sharding import PartitionSpec as P

MESH = pl.DeviceIdType.MESH

ITERS = 3
MARGIN_ROWS = 8
MARGIN_COLS = 8
SENT = 4


courant = -0.4
dispersion = 40.0
continuity = -0.5


def from_behind(value, axis, steps):
    count = lax.axis_size(axis)
    leading, last = (max(0, -steps), min(count, count - steps))
    return lax.ppermute(value, axis, [(source, source + steps) for source in range(leading, last)])


def grow(stacked):
    rows, cols = MARGIN_ROWS, MARGIN_COLS
    above = from_behind(stacked[:, :rows, :], "lat", -1)
    below = from_behind(stacked[:, -rows:, :], "lat", 1)
    width = stacked.shape[2]
    wide = lax.optimization_barrier(jnp.pad(jnp.concatenate([below, stacked, above], axis=1), ((0, 0), (0, 0), (0, 2 * cols))))
    right = from_behind(wide[:, :, :cols], "lon", -1)
    left = from_behind(wide[:, :, width - cols : width], "lon", 1)
    return lax.dynamic_update_slice(wide, jnp.concatenate([right, left], axis=2), (0, 0, width))


def east(field):
    return jnp.roll(field, -1, axis=-1)


def north(field):
    return jnp.pad(field[..., 1:, :], [(0, 0)] * (field.ndim - 2) + [(0, 1), (0, 0)])


def west(field):
    return jnp.roll(field, 1, axis=-1)


def south(field):
    return jnp.pad(field[..., :-1, :], [(0, 0)] * (field.ndim - 2) + [(1, 0), (0, 0)])


def divergence(field):
    return field[0] - west(field[0]) + field[1] - south(field[1])


def operate(field, wet, inverse):
    diverge = divergence(field)
    back = jnp.stack([diverge - east(diverge), diverge - north(diverge)])
    return wet * (inverse * field + back)


def stages_of(sizes):
    return tuple((axis, 1, sizes[axis]) for axis in ("lon", "lat") if sizes[axis] > 1)


def reduce_kernel(stages, local_ref, prev_ref, out_ref, parts, got, send_sem, recv_sem):
    me = {"lat": lax.axis_index("lat"), "lon": lax.axis_index("lon")}

    def partner(axis, stride, members, offset):
        own = me[axis]
        digit = (own // stride) % members
        other = own - digit * stride + ((digit + offset) % members) * stride
        return tuple(other if name == axis else me[name] for name in ("lat", "lon"))

    barrier = pltpu.get_barrier_semaphore()
    greeted = 0
    for axis, stride, members in stages:
        for offset in range(1, members):
            pl.semaphore_signal(barrier, inc=1, device_id=partner(axis, stride, members, offset), device_id_type=MESH)
            greeted += 1
    pl.semaphore_wait(barrier, greeted)

    value = local_ref[0:SENT]
    sent = []
    for stage, (axis, stride, members) in enumerate(stages):
        parts[stage, 0:SENT] = value
        got[stage, 0, 0:SENT] = value
        copies = []
        for offset in range(1, members):
            slot = members - offset
            copy = pltpu.make_async_remote_copy(
                src_ref=parts.at[stage, pl.ds(0, SENT)],
                dst_ref=got.at[stage, slot, pl.ds(0, SENT)],
                send_sem=send_sem.at[stage, offset],
                recv_sem=recv_sem.at[stage, slot],
                device_id=partner(axis, stride, members, offset),
                device_id_type=MESH,
            )
            copy.start()
            copies.append(copy)
        for copy in copies:
            copy.wait_recv()
        sent.extend(copies)
        digit = (me[axis] // stride) % members
        ordered = [got[stage, (member - digit) % members, 0:SENT] for member in range(members)]
        while len(ordered) > 1:
            ordered = [ordered[k] + ordered[k + 1] for k in range(0, len(ordered), 2)]
        value = ordered[0]
    norm, r_ar, r_ap = value[0:1], value[1:2], value[2:3]
    beta = norm / prev_ref[2:3]
    curve = r_ar + 2.0 * beta * r_ap + beta * beta * prev_ref[3:4]
    for copy in sent:
        copy.wait_send()
    out_ref[...] = jnp.zeros(out_ref.shape, out_ref.dtype)
    out_ref[0:1] = norm / curve
    out_ref[1:2] = beta
    out_ref[2:3] = norm
    out_ref[3:4] = curve


def cg_scalars(local, previous):
    sizes = {"lat": lax.axis_size("lat"), "lon": lax.axis_size("lon")}
    stages = stages_of(sizes)
    widest = max(members for _, _, members in stages)
    rows = lax.broadcasted_iota(jnp.int32, (8, 128), 0)
    tile = jnp.zeros((8, 128), jnp.float32)
    for k in range(local.shape[0]):
        tile = jnp.where(rows == k, local[k], tile)
    return pl.pallas_call(
        functools.partial(reduce_kernel, stages),
        out_shape=jax.ShapeDtypeStruct((8, 128), jnp.float32),
        in_specs=[pl.BlockSpec(memory_space=pltpu.VMEM)] * 2,
        out_specs=pl.BlockSpec(memory_space=pltpu.VMEM),
        scratch_shapes=[
            pltpu.VMEM((len(stages), 8, 128), jnp.float32),
            pltpu.VMEM((len(stages), widest, 8, 128), jnp.float32),
            pltpu.SemaphoreType.DMA((len(stages), widest)),
            pltpu.SemaphoreType.DMA((len(stages), widest)),
        ],
        compiler_params=pltpu.CompilerParams(collective_id=0, has_side_effects=True),
    )(tile, previous)


def interior(field):
    rows, cols = MARGIN_ROWS, MARGIN_COLS
    return field[..., rows:-rows, : -2 * cols]


def dots(*pairs):
    return jnp.stack([jnp.sum(interior(x) * interior(y)) for x, y in pairs])


def per_device(surface, bathymetry, land_sea, flux_lon, flux_lat):
    sea = land_sea.astype(jnp.float32)
    grown = grow(jnp.stack([surface, bathymetry, sea, flux_lon, flux_lat]))
    surface_x, bathymetry_x, sea_x = grown[0], grown[1], grown[2]
    wet = jnp.stack([sea_x * east(sea_x), sea_x * north(sea_x)])
    depth = jnp.stack([0.5 * (bathymetry_x + east(bathymetry_x)), 0.5 * (bathymetry_x + north(bathymetry_x))])
    slope = jnp.stack([east(surface_x) - surface_x, north(surface_x) - surface_x])
    start = wet * (grown[3:] - courant * depth * slope)
    inverse = jnp.where(depth > 0, 1.0 / (dispersion * depth * depth), 0.0)
    right_side = wet * inverse * start
    solution = start
    residual = right_side - operate(start, wet, inverse)
    applied = operate(residual, wet, inverse)
    rows = lax.broadcasted_iota(jnp.int32, (8, 128), 0)
    previous = jnp.where(rows == 2, jnp.inf, 0.0).astype(jnp.float32)
    stats = cg_scalars(dots((residual, residual), (residual, applied)), previous)
    direction, image = residual, applied
    for step in range(ITERS):
        alpha = stats[0, 0]
        solution = solution + alpha * direction
        if step == ITERS - 1:
            break
        residual = residual - alpha * image
        applied = operate(residual, wet, inverse)
        stats = cg_scalars(dots((residual, residual), (residual, applied), (residual, image)), stats)
        beta = stats[1, 0]
        direction = residual + beta * direction
        image = applied + beta * image
    surface_next = interior(surface_x - continuity * divergence(solution))
    solution = interior(solution)
    return (surface_next, solution[0], solution[1])


def solution(mesh):
    in_specs = (P("lat", "lon"), P("lat", "lon"), P("lat", "lon"), P("lat", "lon"), P("lat", "lon"))
    out_specs = (P("lat", "lon"), P("lat", "lon"), P("lat", "lon"))
    return jax.shard_map(
        per_device, mesh=mesh, in_specs=in_specs, out_specs=out_specs, check_vma=False
    )
```

```python
import functools

import jax
import jax.numpy as jnp
from jax import lax
from jax.experimental import pallas as pl
from jax.experimental.pallas import tpu as pltpu
from jax.sharding import PartitionSpec as P

MESH = pl.DeviceIdType.MESH

ITERS = 3
MARGIN_ROWS = 8
MARGIN_COLS = 8
SENT = 1


courant = -0.4
dispersion = 40.0
continuity = -0.5


def from_behind(value, axis, steps):
    count = lax.axis_size(axis)
    leading, last = (max(0, -steps), min(count, count - steps))
    return lax.ppermute(value, axis, [(source, source + steps) for source in range(leading, last)])


def grow(stacked):
    rows, cols = MARGIN_ROWS, MARGIN_COLS
    above = from_behind(stacked[:, :rows, :], "lat", -1)
    below = from_behind(stacked[:, -rows:, :], "lat", 1)
    width = stacked.shape[2]
    wide = lax.optimization_barrier(jnp.pad(jnp.concatenate([below, stacked, above], axis=1), ((0, 0), (0, 0), (0, 2 * cols))))
    right = from_behind(wide[:, :, :cols], "lon", -1)
    left = from_behind(wide[:, :, width - cols : width], "lon", 1)
    return lax.dynamic_update_slice(wide, jnp.concatenate([right, left], axis=2), (0, 0, width))


def east(field):
    return jnp.roll(field, -1, axis=-1)


def north(field):
    return jnp.pad(field[..., 1:, :], [(0, 0)] * (field.ndim - 2) + [(0, 1), (0, 0)])


def west(field):
    return jnp.roll(field, 1, axis=-1)


def south(field):
    return jnp.pad(field[..., :-1, :], [(0, 0)] * (field.ndim - 2) + [(1, 0), (0, 0)])


def divergence(field):
    return field[0] - west(field[0]) + field[1] - south(field[1])


def operate(field, wet, inverse):
    diverge = divergence(field)
    back = jnp.stack([diverge - east(diverge), diverge - north(diverge)])
    return wet * (inverse * field + back)


def stages_of(sizes):
    return tuple((axis, 1, sizes[axis]) for axis in ("lon", "lat") if sizes[axis] > 1)


def reduce_kernel(stages, local_ref, prev_ref, out_ref, parts, got, send_sem, recv_sem):
    me = {"lat": lax.axis_index("lat"), "lon": lax.axis_index("lon")}

    def partner(axis, stride, members, offset):
        own = me[axis]
        digit = (own // stride) % members
        other = own - digit * stride + ((digit + offset) % members) * stride
        return tuple(other if name == axis else me[name] for name in ("lat", "lon"))

    barrier = pltpu.get_barrier_semaphore()
    greeted = 0
    for axis, stride, members in stages:
        for offset in range(1, members):
            pl.semaphore_signal(barrier, inc=1, device_id=partner(axis, stride, members, offset), device_id_type=MESH)
            greeted += 1
    pl.semaphore_wait(barrier, greeted)

    value = local_ref[0:SENT]
    for stage, (axis, stride, members) in enumerate(stages):
        parts[stage, 0:SENT] = value
        got[stage, 0, 0:SENT] = value
        copies = []
        for offset in range(1, members):
            slot = members - offset
            copy = pltpu.make_async_remote_copy(
                src_ref=parts.at[stage, pl.ds(0, SENT)],
                dst_ref=got.at[stage, slot, pl.ds(0, SENT)],
                send_sem=send_sem.at[stage, offset],
                recv_sem=recv_sem.at[stage, slot],
                device_id=partner(axis, stride, members, offset),
                device_id_type=MESH,
            )
            copy.start()
            copies.append(copy)
        for copy in copies:
            copy.wait()
        digit = (me[axis] // stride) % members
        ordered = [got[stage, (member - digit) % members, 0:SENT] for member in range(members)]
        while len(ordered) > 1:
            ordered = [ordered[k] + ordered[k + 1] for k in range(0, len(ordered), 2)]
        value = ordered[0]
    norm, r_ar, r_ap = value[:, 0:1], value[:, 1:2], value[:, 2:3]
    beta = jnp.broadcast_to(norm / prev_ref[2:3, 0:1], (1, 128))
    curve = jnp.broadcast_to(r_ar + 2.0 * beta[:, 0:1] * r_ap + beta[:, 0:1] * beta[:, 0:1] * prev_ref[3:4, 0:1], (1, 128))
    norm = jnp.broadcast_to(norm, (1, 128))
    out_ref[...] = jnp.zeros(out_ref.shape, out_ref.dtype)
    out_ref[0:1] = norm / curve
    out_ref[1:2] = beta
    out_ref[2:3] = norm
    out_ref[3:4] = curve


def cg_scalars(local, previous):
    sizes = {"lat": lax.axis_size("lat"), "lon": lax.axis_size("lon")}
    stages = stages_of(sizes)
    widest = max(members for _, _, members in stages)
    rows = lax.broadcasted_iota(jnp.int32, (8, 128), 0)
    lanes = lax.broadcasted_iota(jnp.int32, (8, 128), 1)
    tile = jnp.zeros((8, 128), jnp.float32)
    for k in range(local.shape[0]):
        tile = jnp.where((rows == 0) & (lanes == k), local[k], tile)
    return pl.pallas_call(
        functools.partial(reduce_kernel, stages),
        out_shape=jax.ShapeDtypeStruct((8, 128), jnp.float32),
        in_specs=[pl.BlockSpec(memory_space=pltpu.VMEM)] * 2,
        out_specs=pl.BlockSpec(memory_space=pltpu.VMEM),
        scratch_shapes=[
            pltpu.VMEM((len(stages), 8, 128), jnp.float32),
            pltpu.VMEM((len(stages), widest, 8, 128), jnp.float32),
            pltpu.SemaphoreType.DMA((len(stages), widest)),
            pltpu.SemaphoreType.DMA((len(stages), widest)),
        ],
        compiler_params=pltpu.CompilerParams(collective_id=0, has_side_effects=True),
    )(tile, previous)


def interior(field):
    rows, cols = MARGIN_ROWS, MARGIN_COLS
    return field[..., rows:-rows, : -2 * cols]


def dots(*pairs):
    return jnp.stack([jnp.sum(interior(x) * interior(y)) for x, y in pairs])


def per_device(surface, bathymetry, land_sea, flux_lon, flux_lat):
    sea = land_sea.astype(jnp.float32)
    grown = grow(jnp.stack([surface, bathymetry, sea, flux_lon, flux_lat]))
    surface_x, bathymetry_x, sea_x = grown[0], grown[1], grown[2]
    wet = jnp.stack([sea_x * east(sea_x), sea_x * north(sea_x)])
    depth = jnp.stack([0.5 * (bathymetry_x + east(bathymetry_x)), 0.5 * (bathymetry_x + north(bathymetry_x))])
    slope = jnp.stack([east(surface_x) - surface_x, north(surface_x) - surface_x])
    start = wet * (grown[3:] - courant * depth * slope)
    inverse = jnp.where(depth > 0, 1.0 / (dispersion * depth * depth), 0.0)
    right_side = wet * inverse * start
    solution = start
    residual = right_side - operate(start, wet, inverse)
    applied = operate(residual, wet, inverse)
    rows = lax.broadcasted_iota(jnp.int32, (8, 128), 0)
    previous = jnp.where(rows == 2, jnp.inf, 0.0).astype(jnp.float32)
    stats = cg_scalars(dots((residual, residual), (residual, applied)), previous)
    direction, image = residual, applied
    for step in range(ITERS):
        alpha = stats[0, 0]
        solution = solution + alpha * direction
        if step == ITERS - 1:
            break
        residual = residual - alpha * image
        applied = operate(residual, wet, inverse)
        stats = cg_scalars(dots((residual, residual), (residual, applied), (residual, image)), stats)
        beta = stats[1, 0]
        direction = residual + beta * direction
        image = applied + beta * image
    surface_next = interior(surface_x - continuity * divergence(solution))
    solution = interior(solution)
    return (surface_next, solution[0], solution[1])


def solution(mesh):
    in_specs = (P("lat", "lon"), P("lat", "lon"), P("lat", "lon"), P("lat", "lon"), P("lat", "lon"))
    out_specs = (P("lat", "lon"), P("lat", "lon"), P("lat", "lon"))
    return jax.shard_map(
        per_device, mesh=mesh, in_specs=in_specs, out_specs=out_specs, check_vma=False
    )
```

```python
import functools

import numpy as np

import jax
import jax.numpy as jnp
from jax import lax
from jax.experimental import pallas as pl
from jax.experimental.pallas import tpu as pltpu
from jax.sharding import PartitionSpec as P

MESH = pl.DeviceIdType.MESH

ITERS = 3
MARGIN_ROWS = 8
MARGIN_COLS = 8
SENT = 4


courant = -0.4
dispersion = 40.0
continuity = -0.5


def from_behind(value, axis, steps):
    count = lax.axis_size(axis)
    leading, last = (max(0, -steps), min(count, count - steps))
    return lax.ppermute(value, axis, [(source, source + steps) for source in range(leading, last)])


def grow(stacked):
    rows, cols = MARGIN_ROWS, MARGIN_COLS
    above = from_behind(stacked[:, :rows, :], "lat", -1)
    below = from_behind(stacked[:, -rows:, :], "lat", 1)
    width = stacked.shape[2]
    wide = lax.optimization_barrier(jnp.pad(jnp.concatenate([below, stacked, above], axis=1), ((0, 0), (0, 0), (0, 2 * cols))))
    right = from_behind(wide[:, :, :cols], "lon", -1)
    left = from_behind(wide[:, :, width - cols : width], "lon", 1)
    return lax.dynamic_update_slice(wide, jnp.concatenate([right, left], axis=2), (0, 0, width))


def east(field):
    return jnp.roll(field, -1, axis=-1)


def north(field):
    return jnp.pad(field[..., 1:, :], [(0, 0)] * (field.ndim - 2) + [(0, 1), (0, 0)])


def west(field):
    return jnp.roll(field, 1, axis=-1)


def south(field):
    return jnp.pad(field[..., :-1, :], [(0, 0)] * (field.ndim - 2) + [(1, 0), (0, 0)])


def divergence(field):
    return field[0] - west(field[0]) + field[1] - south(field[1])


def operate(field, wet, inverse):
    diverge = divergence(field)
    back = jnp.stack([diverge - east(diverge), diverge - north(diverge)])
    return wet * (inverse * field + back)


def stages_of(sizes):
    return tuple((axis, 1, sizes[axis]) for axis in ("lon", "lat") if sizes[axis] > 1)


def reduce_kernel(stages, local_ref, prev_ref, out_ref, parts, got, send_sem, recv_sem):
    me = {"lat": lax.axis_index("lat"), "lon": lax.axis_index("lon")}

    def partner(axis, stride, members, offset):
        own = me[axis]
        digit = (own // stride) % members
        other = own - digit * stride + ((digit + offset) % members) * stride
        return tuple(other if name == axis else me[name] for name in ("lat", "lon"))

    barrier = pltpu.get_barrier_semaphore()
    greeted = 0
    for axis, stride, members in stages:
        for offset in range(1, members):
            pl.semaphore_signal(barrier, inc=1, device_id=partner(axis, stride, members, offset), device_id_type=MESH)
            greeted += 1
    pl.semaphore_wait(barrier, greeted)

    value = local_ref[0:SENT]
    for stage, (axis, stride, members) in enumerate(stages):
        parts[stage, 0:SENT] = value
        got[stage, 0, 0:SENT] = value
        copies = []
        for offset in range(1, members):
            slot = members - offset
            copy = pltpu.make_async_remote_copy(
                src_ref=parts.at[stage, pl.ds(0, SENT)],
                dst_ref=got.at[stage, slot, pl.ds(0, SENT)],
                send_sem=send_sem.at[stage, offset],
                recv_sem=recv_sem.at[stage, slot],
                device_id=partner(axis, stride, members, offset),
                device_id_type=MESH,
            )
            copy.start()
            copies.append(copy)
        for copy in copies:
            copy.wait()
        digit = (me[axis] // stride) % members
        ordered = [got[stage, (member - digit) % members, 0:SENT] for member in range(members)]
        while len(ordered) > 1:
            ordered = [ordered[k] + ordered[k + 1] for k in range(0, len(ordered), 2)]
        value = ordered[0]
    norm, r_ar, r_ap = value[0:1], value[1:2], value[2:3]
    beta = norm / prev_ref[2:3]
    curve = r_ar + 2.0 * beta * r_ap + beta * beta * prev_ref[3:4]
    out_ref[...] = jnp.zeros(out_ref.shape, out_ref.dtype)
    out_ref[0:1] = norm / curve
    out_ref[1:2] = beta
    out_ref[2:3] = norm
    out_ref[3:4] = curve


def cg_scalars(local, previous):
    sizes = {"lat": lax.axis_size("lat"), "lon": lax.axis_size("lon")}
    stages = stages_of(sizes)
    widest = max(members for _, _, members in stages)
    rows = lax.broadcasted_iota(jnp.int32, (8, 128), 0)
    tile = jnp.zeros((8, 128), jnp.float32)
    for k in range(local.shape[0]):
        tile = jnp.where(rows == k, local[k], tile)
    return pl.pallas_call(
        functools.partial(reduce_kernel, stages),
        out_shape=jax.ShapeDtypeStruct((8, 128), jnp.float32),
        in_specs=[pl.BlockSpec(memory_space=pltpu.VMEM)] * 2,
        out_specs=pl.BlockSpec(memory_space=pltpu.VMEM),
        scratch_shapes=[
            pltpu.VMEM((len(stages), 8, 128), jnp.float32),
            pltpu.VMEM((len(stages), widest, 8, 128), jnp.float32),
            pltpu.SemaphoreType.DMA((len(stages), widest)),
            pltpu.SemaphoreType.DMA((len(stages), widest)),
        ],
        compiler_params=pltpu.CompilerParams(collective_id=0, has_side_effects=True),
    )(tile, previous)


def interior(field):
    rows, cols = MARGIN_ROWS, MARGIN_COLS
    return field[..., rows:-rows, : -2 * cols]


def dots(*pairs):
    return jnp.stack([jnp.sum(interior(x) * interior(y)) for x, y in pairs])


def per_device(surface, bathymetry, land_sea, flux_lon, flux_lat):
    sea = land_sea.astype(jnp.float32)
    grown = grow(jnp.stack([surface, bathymetry, sea, flux_lon, flux_lat]))
    surface_x, bathymetry_x, sea_x = grown[0], grown[1], grown[2]
    wet = jnp.stack([sea_x * east(sea_x), sea_x * north(sea_x)])
    depth = jnp.stack([0.5 * (bathymetry_x + east(bathymetry_x)), 0.5 * (bathymetry_x + north(bathymetry_x))])
    slope = jnp.stack([east(surface_x) - surface_x, north(surface_x) - surface_x])
    start = wet * (grown[3:] - courant * depth * slope)
    inverse = jnp.where(depth > 0, 1.0 / (dispersion * depth * depth), 0.0)
    right_side = wet * inverse * start
    solution = start
    residual = right_side - operate(start, wet, inverse)
    applied = operate(residual, wet, inverse)
    previous = np.zeros((8, 128), np.float32)
    previous[2] = np.inf
    previous = jnp.asarray(previous)
    stats = cg_scalars(dots((residual, residual), (residual, applied)), previous)
    direction, image = residual, applied
    for step in range(ITERS):
        alpha = stats[0, 0]
        solution = solution + alpha * direction
        if step == ITERS - 1:
            break
        residual = residual - alpha * image
        applied = operate(residual, wet, inverse)
        stats = cg_scalars(dots((residual, residual), (residual, applied), (residual, image)), stats)
        beta = stats[1, 0]
        direction = residual + beta * direction
        image = applied + beta * image
    surface_next = interior(surface_x - continuity * divergence(solution))
    solution = interior(solution)
    return (surface_next, solution[0], solution[1])


def solution(mesh):
    in_specs = (P("lat", "lon"), P("lat", "lon"), P("lat", "lon"), P("lat", "lon"), P("lat", "lon"))
    out_specs = (P("lat", "lon"), P("lat", "lon"), P("lat", "lon"))
    return jax.shard_map(
        per_device, mesh=mesh, in_specs=in_specs, out_specs=out_specs, check_vma=False
    )
```
